128 devices in a mesh: frame: 4 (over x), pix: 32 (over y, z, core).
Axes of the slice: x: 4, y: 4, z: 4, core: 2. Of those that a mesh axis runs over, the one named last changes fastest.
Arguments:
- frames: bfloat16 [128, 4, 512, 512], P('frame', None, 'pix'), may hold values from -26 to 26
- prev_fg: bfloat16 [128, 4, 512, 512], P('frame', None, 'pix'), may hold values from -3 to 3
- depth_valid: int32 [128, 512, 512], P('frame', 'pix'), may hold values 0 or 1
- sketch: float32 [128, 64], replicated, may hold values from -0.5 to 0.5
- tv_weight: float32 [4], replicated, may hold values from 0.1 to 1
Outputs:
- background: bfloat16 [128, 4, 512, 512], P('frame', None, 'pix')
- foreground: bfloat16 [128, 4, 512, 512], P('frame', None, 'pix')
The draws below stay inside these ranges and needn't reach their ends.
All inputs are finite; a program needn't handle non-finite values. No bound on the sum of `depth_valid` on one device may be relied on, other than what follows from the above.
Results may differ from the reference program's by a relative error of at most 0.012.
The reference program's roundings to bfloat16 on the way count: a program that leaves them out, or rounds other values in their place, can miss the bound.
Values may be sent and summed in bfloat16 or wider, within the bound.
A program may use at most 64 MiB of HBM per device.

```python
import math
import jax
import jax.numpy as jnp
from jax import lax

CH = 4
RANK = 64
COLS = 512
POWER = 3
NSWEEP = 5
FRAMES = 128
HEIGHT = 512


def draw_frames(key, part):
    subkeys = jax.random.split(key, 8)
    shape = (FRAMES, CH, HEIGHT, COLS)
    pixel_shape = (1, CH, HEIGHT, COLS)
    level = jnp.exp(jax.random.uniform(subkeys[0], (FRAMES, 1, 1, 1), jnp.float32, math.log(0.3), math.log(3.0)))
    row_pos = lax.broadcasted_iota(jnp.float32, (1, 1, HEIGHT, 1), 2)
    rise = jnp.sqrt(1.0 + 2.0 * row_pos / max(HEIGHT - 1, 1))
    moments = lax.broadcasted_iota(jnp.float32, (FRAMES, 1, 1, 1), 0)
    exponent = 2.0
    motion = 0.5 * jax.random.truncated_normal(subkeys[1], -4.0, 4.0, shape, jnp.float32)
    for wave in range(2):
        frequency = math.pi * jax.random.uniform(subkeys[2 + 3 * wave], pixel_shape, jnp.float32) ** exponent
        phase = jax.random.uniform(subkeys[3 + 3 * wave], pixel_shape, jnp.float32, -math.pi, math.pi)
        amplitude = jax.random.uniform(subkeys[4 + 3 * wave], pixel_shape, jnp.float32, 0.5, 1.5)
        motion = motion + amplitude * jnp.cos(frequency * moments + phase)
    return (motion * level * rise).astype(jnp.bfloat16)


def place_ends(entries, own_key, smallest, top_value):
    place = [jax.random.randint(jax.random.fold_in(own_key, axis), (), 0, length) for axis, length in enumerate(entries.shape)]
    longest = entries.shape.index(max(entries.shape))
    beside = place[:longest] + [(place[longest] + 1) % entries.shape[longest]] + place[longest + 1:]
    return entries.at[tuple(place)].set(smallest).at[tuple(beside)].set(top_value)


def steps_of(own_key, shape, cuts, low, top_value):
    def one(dim, parts):
        steps = jax.random.uniform(jax.random.fold_in(jax.random.fold_in(own_key, 6), dim), (parts,), jnp.float32, low / len(cuts), top_value / len(cuts))
        return jnp.repeat(jnp.exp(steps), shape[dim] // parts).reshape((-1,) + (1,) * (len(shape) - dim - 1))

    loudness = one(*cuts[0])
    for cut in cuts[1:]:
        loudness = loudness * one(*cut)
    return loudness


def centred(stream_key, dims, width, bound, shards=(), held_as=jnp.bfloat16):
    loudness = steps_of(stream_key, dims, shards, -0.22, 0.18) if shards else 1.0
    drawn = jax.random.normal(stream_key, dims, jnp.float32) * width * loudness
    return jnp.minimum(jnp.maximum(drawn, -bound), bound).astype(held_as)


def setup_inputs(seed: int = 0) -> dict:
    streams_of = jax.random.split(jax.random.key(seed), 6)
    frames = draw_frames(jax.random.fold_in(streams_of[5], 71), 0)
    prev_fg = centred(streams_of[1], (FRAMES, CH, HEIGHT, COLS), 0.5, 3.0, ((0, 4), (2, 32)))
    depth_valid = place_ends((jax.random.randint(streams_of[2], (FRAMES, HEIGHT, COLS), 0, 8) < 7).astype(jnp.int32), jax.random.fold_in(streams_of[2], 1), 0, 1)
    sketch = centred(streams_of[3], (FRAMES, RANK), FRAMES ** -0.5, 0.5, (), jnp.float32)
    tv_weight = jnp.clip(jnp.exp(jax.random.uniform(streams_of[4], (CH,), jnp.float32, math.log(0.1), math.log(1.0))), 0.1, 1.0)
    return {"frames": frames, "prev_fg": prev_fg, "depth_valid": depth_valid, "sketch": sketch, "tv_weight": tv_weight}


STEP_SIZE = 0.125

def exact_dot(left, right):
    return jnp.dot(left, right, precision=lax.Precision.HIGHEST)

def mixing_matrix(gram, sketch):
    basis = sketch
    for turn in range(POWER):
        image = exact_dot(gram, basis)
        factor = jnp.linalg.cholesky(exact_dot(basis.T, image))
        basis = lax.linalg.triangular_solve(factor, image, left_side=False, lower=True, transpose_a=True)
    image = exact_dot(gram, basis)
    factor = jnp.linalg.cholesky(exact_dot(basis.T, image))
    middle = lax.linalg.triangular_solve(factor, exact_dot(basis.T, gram), left_side=True, lower=True)
    coeffs = lax.linalg.triangular_solve(factor, middle, left_side=True, lower=True, transpose_a=True)
    return exact_dot(basis, coeffs)

def dual_update(first, second, down, across, step):
    size = jnp.sqrt(down * down + across * across)
    scale = 1.0 + step * size
    return ((first - step * down) / scale, (second - step * across) / scale)

def reference(frames, prev_fg, depth_valid, sketch, tv_weight):
    chan_ids = lax.broadcasted_iota(jnp.int32, (1, CH, 1, 1), 1)
    depth_ok = depth_valid[:, None, :, :].astype(jnp.float32)
    valid = jnp.where(chan_ids == CH - 1, depth_ok, jnp.float32(1.0))
    resid = ((frames.astype(jnp.float32) - prev_fg.astype(jnp.float32)) * valid).astype(jnp.bfloat16)
    flat = resid.reshape(FRAMES, CH * HEIGHT * COLS)
    gram = jnp.dot(flat.astype(jnp.float32), flat.T.astype(jnp.float32), preferred_element_type=jnp.float32) / (CH * HEIGHT * COLS)
    mixing = mixing_matrix(gram, sketch)
    back = jnp.dot(mixing.astype(jnp.bfloat16).T.astype(jnp.float32), flat.astype(jnp.float32), preferred_element_type=jnp.float32)
    back = back.reshape(FRAMES, CH, HEIGHT, COLS)
    background = back.astype(jnp.bfloat16)
    rounded = lax.optimization_barrier(background).astype(jnp.float32)
    source = (frames.astype(jnp.float32) - rounded) * valid
    lam = tv_weight.reshape(CH, 1, 1)
    step = STEP_SIZE / lam
    last_row = lax.broadcasted_iota(jnp.int32, (1, HEIGHT, 1), 1) == HEIGHT - 1
    last_col = lax.broadcasted_iota(jnp.int32, (1, 1, COLS), 2) == COLS - 1

    def divergence(first, second):
        prev_rows = jnp.pad(first[:, :-1, :], ((0, 0), (1, 0), (0, 0)))
        prev_cols = jnp.pad(second[:, :, :-1], ((0, 0), (0, 0), (1, 0)))
        return first - prev_rows + (second - prev_cols)

    def one_frame(image):
        first = jnp.zeros_like(image)
        second = jnp.zeros_like(image)
        for sweep in range(NSWEEP):
            smooth = image - lam * divergence(first, second)
            next_rows = jnp.pad(smooth[:, 1:, :], ((0, 0), (0, 1), (0, 0)))
            next_cols = jnp.pad(smooth[:, :, 1:], ((0, 0), (0, 0), (0, 1)))
            down = jnp.where(last_row, 0.0, next_rows - smooth)
            across = jnp.where(last_col, 0.0, next_cols - smooth)
            first, second = dual_update(first, second, down, across, step)
        return image - lam * divergence(first, second)
    foreground = lax.map(one_frame, source).astype(jnp.bfloat16)
    return (background, foreground)
```

```python
import functools

import jax
import jax.numpy as jnp
from jax import lax
from jax.experimental import pallas as pl
from jax.experimental.pallas import tpu as pltpu
from jax.sharding import PartitionSpec as P

POWER = 3
NSWEEP = 5
STEP_SIZE = 0.125
MESH = pl.DeviceIdType.MESH
VMEM = pltpu.VMEM
SIDE = 4
BF16 = jnp.bfloat16
F32 = jnp.float32


def in_vmem(count):
    return [pl.BlockSpec(memory_space=pltpu.VMEM)] * count


def wrap(value, size):
    return lax.rem(value + size, size)


def place():
    x = lax.axis_index("frame")
    strip = lax.axis_index("pix")
    return x, strip, lax.div(strip, 8), lax.rem(lax.div(strip, 2), 4), lax.rem(strip, 2)


def greet(partners):
    barrier = pltpu.get_barrier_semaphore()
    for partner in partners:
        pl.semaphore_signal(barrier, inc=1, device_id=partner, device_id_type=MESH)
    pl.semaphore_wait(barrier, len(partners))


def swap_along_x(x, strip, src, dst, relay, local_sem, send_sem, recv_sem):
    right, left, opposite = wrap(x + 1, SIDE), wrap(x - 1, SIDE), wrap(x + 2, SIDE)
    half = src.shape[-1] // 2
    low, high = pl.ds(0, half), pl.ds(half, half)

    def copy(source, target, slot, to):
        return pltpu.make_async_remote_copy(
            src_ref=source,
            dst_ref=target,
            send_sem=send_sem.at[slot],
            recv_sem=recv_sem.at[slot],
            device_id=(to, strip),
            device_id_type=MESH,
        )

    out_low = copy(src.at[opposite, :, low], relay.at[0], 0, right)
    out_high = copy(src.at[opposite, :, high], relay.at[1], 1, left)
    to_right = copy(src.at[right], dst.at[x], 2, right)
    to_left = copy(src.at[left], dst.at[x], 3, left)
    out_low.start()
    out_high.start()
    to_right.start()
    to_left.start()
    mine = pltpu.make_async_copy(src.at[x], dst.at[x], local_sem)
    mine.start()
    out_low.wait_recv()
    on_low = copy(relay.at[0], dst.at[left, :, low], 4, right)
    on_low.start()
    out_high.wait_recv()
    on_high = copy(relay.at[1], dst.at[right, :, high], 5, left)
    on_high.start()
    mine.wait()
    copy(src.at[right], dst.at[left], 2, right).wait_recv()
    copy(src.at[left], dst.at[right], 3, left).wait_recv()
    copy(relay.at[0], dst.at[opposite, :, low], 4, right).wait_recv()
    copy(relay.at[1], dst.at[opposite, :, high], 5, left).wait_recv()
    for sent in (out_low, out_high, to_right, to_left, on_low, on_high):
        sent.wait_send()


def gram_kernel(
    resid, swapped, gram, relay, part, pieces, in_y, in_z, total,
    local_sem, swap_send, swap_recv, first_send, first_recv, y_send, y_recv, z_send, z_recv,
    last_send, last_recv,
):
    x, strip, y, z, core = place()
    group = x * 2 + core

    def of_group(k):
        return (lax.div(k, 2), strip - core + lax.rem(k, 2))

    def of_y(k):
        return (x, (k * 4 + z) * 2 + core)

    def of_z(k):
        return (x, (y * 4 + k) * 2 + core)

    partners = [of_group(wrap(group + k, 8)) for k in range(1, 8)]
    partners += [of_y(wrap(y + k, 4)) for k in range(1, 4)]
    partners += [of_z(wrap(z + k, 4)) for k in range(1, 4)]
    greet(partners)
    swap_along_x(x, strip, resid, swapped, relay, local_sem, swap_send, swap_recv)

    frames = part.shape[0] * part.shape[1]
    pixels = swapped.shape[-1]
    chunk = 1024

    def add(step, so_far):
        cols = pl.ds(pl.multiple_of(step * chunk, chunk), chunk)
        block = swapped[:, :, cols].reshape(frames, chunk)
        return so_far + lax.dot_general(
            block, block, (((1,), (1,)), ((), ())), preferred_element_type=F32
        )

    partial = lax.fori_loop(0, pixels // chunk, add, jnp.zeros((frames, frames), F32))
    part[...] = partial.reshape(part.shape)

    def exchange(index, size, where, source_of, buffer, send_sem, recv_sem):
        copies = []
        for k in range(1, size):
            to = wrap(index + k, size)
            copies.append(
                pltpu.make_async_remote_copy(
                    src_ref=source_of(to),
                    dst_ref=buffer.at[index],
                    send_sem=send_sem.at[k],
                    recv_sem=recv_sem.at[k],
                    device_id=where(to),
                    device_id_type=MESH,
                )
            )
        for copy in copies:
            copy.start()
        return copies

    def arrive(index, size, where, source_of, buffer, send_sem, recv_sem, copies):
        for k in range(1, size):
            pltpu.make_async_remote_copy(
                src_ref=source_of(wrap(index + k, size)),
                dst_ref=buffer.at[wrap(index - k, size)],
                send_sem=send_sem.at[k],
                recv_sem=recv_sem.at[k],
                device_id=where(wrap(index + k, size)),
                device_id_type=MESH,
            ).wait_recv()
        for copy in copies:
            copy.wait_send()

    def added(buffer, size):
        out = buffer[0]
        for k in range(1, size):
            out = out + buffer[k]
        return out

    args = (group, 8, of_group, lambda k: part.at[k], pieces, first_send, first_recv)
    copies = exchange(*args)
    pieces[group] = part[group]
    arrive(*args, copies)
    in_y[y] = added(pieces, 8)

    args = (y, 4, of_y, lambda k: in_y.at[y], in_y, y_send, y_recv)
    arrive(*args, exchange(*args))
    in_z[z] = added(in_y, 4)

    args = (z, 4, of_z, lambda k: in_z.at[z], in_z, z_send, z_recv)
    arrive(*args, exchange(*args))
    total[group] = added(in_z, 4)

    args = (group, 8, of_group, lambda k: total.at[group], total, last_send, last_recv)
    arrive(*args, exchange(*args))
    gram[...] = total[...].reshape(gram.shape)


def gram_of(resid):
    chans, count, pixels = resid.shape
    frames = count * SIDE
    rows = frames // 8
    dma = pltpu.SemaphoreType.DMA
    return pl.pallas_call(
        gram_kernel,
        out_shape=(
            jax.ShapeDtypeStruct((SIDE, count, pixels), BF16),
            jax.ShapeDtypeStruct((frames, frames), F32),
        ),
        in_specs=in_vmem(1),
        out_specs=tuple(in_vmem(2)),
        scratch_shapes=[
            VMEM((2, count, pixels // 2), BF16),
            VMEM((8, rows, frames), F32),
            VMEM((8, rows, frames), F32),
            VMEM((4, rows, frames), F32),
            VMEM((4, rows, frames), F32),
            VMEM((8, rows, frames), F32),
            dma,
            dma((6,)), dma((6,)),
            dma((8,)), dma((8,)),
            dma((4,)), dma((4,)),
            dma((4,)), dma((4,)),
            dma((8,)), dma((8,)),
        ],
        compiler_params=pltpu.CompilerParams(
            collective_id=0, has_side_effects=True, vmem_limit_bytes=40 << 20
        ),
        name="gram",
    )(resid)


def exact(left, right, dims):
    return lax.dot_general(
        left, right, (dims, ((), ())), precision=lax.Precision.HIGHEST, preferred_element_type=F32
    )


def lower_solve(square, sides):
    size = square.shape[0]
    blocks = size // 8
    sub = lax.broadcasted_iota(jnp.int32, (8, 128), 0)
    tiles = [square[8 * i : 8 * i + 8, :] for i in range(blocks)]
    hands = [[side[8 * i : 8 * i + 8, :] for i in range(blocks)] for side in sides]
    solved = [[] for _ in sides]
    for b in range(blocks):
        cols = [
            [
                jnp.broadcast_to(tiles[i][:, 8 * b + t : 8 * b + t + 1], (8, 128))
                if i >= b
                else None
                for i in range(blocks)
            ]
            for t in range(8)
        ]
        pivot = [
            [
                jnp.broadcast_to(cols[t][b][u : u + 1, :], (8, 128)) if u >= t else None
                for u in range(8)
            ]
            for t in range(8)
        ]
        rate = []
        low = [[None] * 8 for _ in range(8)]
        for t in range(8):
            rate.append(lax.rsqrt(pivot[t][t]))
            for u in range(t + 1, 8):
                low[u][t] = pivot[t][u] * rate[t]
            for u in range(t + 1, 8):
                for v in range(u, 8):
                    pivot[u][v] = pivot[u][v] - low[u][t] * low[v][t]

        def reduced(rows):
            done = []
            for t in range(8):
                value = rows[t]
                for s in range(t):
                    value = value - done[s] * low[t][s][:, : value.shape[1]]
                done.append(value * rate[t][:, : value.shape[1]])
            return done

        below = {i: reduced([cols[t][i] for t in range(8)]) for i in range(b + 1, blocks)}
        if b + 1 < blocks:
            across = reduced(
                [jnp.broadcast_to(tiles[b][t : t + 1, :], (8, size)) for t in range(8)]
            )
            for i in range(b + 1, blocks):
                for t in range(8):
                    tiles[i] = tiles[i] - below[i][t][:, :size] * across[t]
        for hand, out in zip(hands, solved):
            rows = reduced([jnp.broadcast_to(hand[b][t : t + 1, :], (8, 128)) for t in range(8)])
            tile = rows[0]
            for t in range(1, 8):
                tile = jnp.where(sub == t, rows[t], tile)
            out.append(tile)
            for i in range(b + 1, blocks):
                for t in range(8):
                    hand[i] = hand[i] - below[i][t] * rows[t]
    return [jnp.concatenate(out, axis=0) for out in solved]


def mixing_kernel(nval, gram_ref, sketch_ref, mixing_ref, gram_sc, basis_sc):
    gram_sc[...] = gram_ref[...] * (1.0 / nval)
    basis_sc[...] = sketch_ref[...]

    def turn(step, carry):
        basis = basis_sc[...]
        image = exact(basis, gram_sc[...], ((1,), (1,)))
        square = exact(basis, image, ((1,), (1,)))
        basis_sc[...] = lower_solve(square, [image])[0]
        return carry

    lax.fori_loop(0, POWER, turn, 0)
    basis = basis_sc[...]
    image = exact(basis, gram_sc[...], ((1,), (0,)))
    square = exact(basis, image, ((1,), (1,)))
    left, right = lower_solve(square, [basis, image])
    mixing_ref[...] = exact(right, left, ((0,), (0,))).astype(BF16)


def mixing_of(gram, sketch, nval):
    frames, rank = sketch.shape
    return pl.pallas_call(
        functools.partial(mixing_kernel, nval),
        out_shape=jax.ShapeDtypeStruct((frames, frames), BF16),
        in_specs=in_vmem(2),
        out_specs=in_vmem(1)[0],
        scratch_shapes=[VMEM((frames, frames), F32), VMEM((rank, frames), F32)],
        name="mixing",
    )(gram, sketch.T)


def back_kernel(
    swapped, weights, frames, valid, back, above, below,
    made, relay, top, bottom, local_sem, swap_send, swap_recv, halo_send, halo_recv,
):
    x, strip, _, _, _ = place()
    strips = lax.axis_size("pix")
    up, down = wrap(strip - 1, strips), wrap(strip + 1, strips)
    greet([(wrap(x + 1, SIDE), strip), (wrap(x - 1, SIDE), strip), (x, up), (x, down)])
    side, count, pixels = swapped.shape
    chunk = 1024
    mix = weights[...]

    def multiply(step, carry):
        cols = pl.ds(pl.multiple_of(step * chunk, chunk), chunk)
        block = swapped[:, :, cols].reshape(side * count, chunk)
        out = jnp.dot(mix, block, preferred_element_type=F32)
        made[:, :, cols] = out.astype(BF16).reshape(side, count, chunk)
        return carry

    lax.fori_loop(0, pixels // chunk, multiply, 0)
    swap_along_x(x, strip, made, back, relay, local_sem, swap_send, swap_recv)
    width = top.shape[-1]
    for chan in range(side):
        for target, start in ((top, 0), (bottom, pixels - width)):
            cols = slice(start, start + width)
            source = frames[chan, :, cols].astype(F32) - back[chan, :, cols].astype(F32)
            if chan == side - 1:
                source = source * valid[:, cols].astype(F32)
            target[chan] = source.astype(BF16)
    copies = []
    for k, (source, target, to) in enumerate(((top, below, up), (bottom, above, down))):
        copies.append(
            pltpu.make_async_remote_copy(
                src_ref=source,
                dst_ref=target,
                send_sem=halo_send.at[k],
                recv_sem=halo_recv.at[k],
                device_id=(x, to),
                device_id_type=MESH,
            )
        )
    for copy in copies:
        copy.start()
    for copy in copies:
        copy.wait()


def back_of(swapped, weights, frames, valid, cols):
    side, count, pixels = swapped.shape
    dma = pltpu.SemaphoreType.DMA
    halo = (side, count, NSWEEP * cols)
    return pl.pallas_call(
        back_kernel,
        out_shape=(
            jax.ShapeDtypeStruct(swapped.shape, BF16),
            jax.ShapeDtypeStruct(halo, BF16),
            jax.ShapeDtypeStruct(halo, BF16),
        ),
        in_specs=in_vmem(4),
        out_specs=tuple(in_vmem(3)),
        scratch_shapes=[
            VMEM(swapped.shape, BF16),
            VMEM((2, count, pixels // 2), BF16),
            VMEM(halo, BF16),
            VMEM(halo, BF16),
            dma,
            dma((6,)), dma((6,)),
            dma((2,)), dma((2,)),
        ],
        compiler_params=pltpu.CompilerParams(
            collective_id=1, has_side_effects=True, vmem_limit_bytes=40 << 20
        ),
        name="back",
    )(swapped, weights, frames, valid)


def tv_kernel(
    strips, strip_ref, lam_ref, frames, back, valid, above, below, out, source, first, second
):
    chan = pl.program_id(0)
    last = pl.num_programs(0) - 1
    lam = lam_ref[chan]
    step = STEP_SIZE / lam
    strip = strip_ref[0]
    halo = NSWEEP
    span, lines, cols = source.shape
    rows = span - 2 * halo
    height = strips * rows

    for r in range(halo):
        source[r] = above[0, :, r * cols : (r + 1) * cols].astype(F32)
        source[halo + rows + r] = below[0, :, r * cols : (r + 1) * cols].astype(F32)
    for r in range(rows):
        where = slice(r * cols, (r + 1) * cols)
        ok = jnp.where(chan == last, valid[:, where].astype(F32), 1.0)
        source[halo + r] = (
            frames[0, :, where].astype(F32) - back[0, :, where].astype(F32)
        ) * ok

    inner_col = (
        lax.broadcasted_iota(jnp.int32, (lines, cols), 1) < cols - 1
    )

    def update(r, smooth, after, old_first, old_second):
        row = strip * rows + r - halo
        inside = jnp.where((row >= 0) & (row < height - 1), F32(1.0), F32(0.0))
        down = (after - smooth) * inside
        across = jnp.where(inner_col, pltpu.roll(smooth, cols - 1, 1) - smooth, 0.0)
        square = down * down + across * across
        size = square * lax.rsqrt(jnp.maximum(square, 1e-37))
        rate = 1.0 / (1.0 + step * size)
        new_first = -step * down if old_first is None else old_first - step * down
        new_second = -step * across if old_second is None else old_second - step * across
        first[r] = new_first * rate
        second[r] = new_second * rate

    def start(r, smooth):
        after = source[r + 1]
        update(r, smooth, after, None, None)
        return after

    lax.fori_loop(0, span - 1, start, source[0])

    def image(r, up, here, beside):
        turn = here - up + (beside - pltpu.roll(beside, 1, 1))
        return source[r] - lam * turn

    def line(r, carry):
        smooth, here, beside = carry
        next_first, next_second = first[r + 1], second[r + 1]
        after = image(r + 1, here, next_first, next_second)
        update(r, smooth, after, here, beside)
        return after, next_first, next_second

    for sweep in range(1, NSWEEP):
        here, beside = first[sweep], second[sweep]
        smooth = image(sweep, first[sweep - 1], here, beside)
        lax.fori_loop(sweep, span - 1 - sweep, line, (smooth, here, beside))
    for r in range(rows):
        value = image(halo + r, first[halo + r - 1], first[halo + r], second[halo + r])
        out[0, :, r * cols : (r + 1) * cols] = value.astype(BF16)


def foreground_of(frames, back, valid, above, below, lam, strip, strips, cols):
    chans, count, pixels = frames.shape
    lines = 16
    rows = pixels // cols
    span = rows + 2 * NSWEEP
    whole = pl.BlockSpec((1, lines, pixels), lambda c, f, *_: (c, f, 0))
    edge = pl.BlockSpec((1, lines, NSWEEP * cols), lambda c, f, *_: (c, f, 0))
    scalar = pl.BlockSpec(memory_space=pltpu.SMEM)
    return pl.pallas_call(
        functools.partial(tv_kernel, strips),
        grid=(chans, count // lines),
        out_shape=jax.ShapeDtypeStruct(frames.shape, BF16),
        in_specs=[
            scalar,
            scalar,
            whole,
            whole,
            pl.BlockSpec((lines, pixels), lambda c, f: (f, 0)),
            edge,
            edge,
        ],
        out_specs=whole,
        scratch_shapes=[VMEM((span, lines, cols), F32)] * 3,
        compiler_params=pltpu.CompilerParams(vmem_limit_bytes=40 << 20),
        name="tv",
    )(strip, lam, frames, back, valid, above, below)


def local(frames, prev_fg, depth_valid, sketch, tv_weight):
    count, chans, rows, cols = frames.shape
    strips = lax.axis_size("pix")
    nval = chans * rows * strips * cols
    chan_ids = lax.broadcasted_iota(jnp.int32, (1, chans, 1, 1), 1)
    depth_ok = depth_valid[:, None, :, :].astype(F32)
    valid = jnp.where(chan_ids == chans - 1, depth_ok, F32(1.0))
    resid = ((frames.astype(F32) - prev_fg.astype(F32)) * valid).astype(BF16)

    def flat(value):
        return value.transpose(1, 0, 2, 3).reshape(chans, count, rows * cols)

    resid, frames = flat(resid), flat(frames)
    ok = depth_valid.astype(BF16).reshape(count, rows * cols)
    swapped, gram = gram_of(resid)
    weights = mixing_of(gram, sketch, nval)
    back, above, below = back_of(swapped, weights, frames, ok, cols)
    strip = lax.axis_index("pix").reshape(1)
    fore = foreground_of(frames, back, ok, above, below, tv_weight, strip, strips, cols)

    def unflat(value):
        return value.reshape(chans, count, rows, cols).transpose(1, 0, 2, 3)

    return unflat(back), unflat(fore)


def solution(mesh):
    placed = (
        P("frame", None, "pix", None),
        P("frame", None, "pix", None),
        P("frame", "pix", None),
        P(),
        P(),
    )
    return jax.shard_map(
        local,
        mesh=mesh,
        in_specs=placed,
        out_specs=(P("frame", None, "pix", None), P("frame", None, "pix", None)),
        check_vma=False,
    )
```

```python
import functools

import jax
import jax.numpy as jnp
from jax import lax
from jax.experimental import pallas as pl
from jax.experimental.pallas import tpu as pltpu
from jax.sharding import PartitionSpec as P

POWER = 3
NSWEEP = 5
STEP_SIZE = 0.125
MESH = pl.DeviceIdType.MESH
VMEM = pltpu.VMEM
SIDE = 4
BF16 = jnp.bfloat16
F32 = jnp.float32


def in_vmem(count):
    return [pl.BlockSpec(memory_space=pltpu.VMEM)] * count


def wrap(value, size):
    return lax.rem(value + size, size)


def place():
    x = lax.axis_index("frame")
    strip = lax.axis_index("pix")
    return x, strip, lax.div(strip, 8), lax.rem(lax.div(strip, 2), 4), lax.rem(strip, 2)


def greet(partners):
    barrier = pltpu.get_barrier_semaphore()
    for partner in partners:
        pl.semaphore_signal(barrier, inc=1, device_id=partner, device_id_type=MESH)
    pl.semaphore_wait(barrier, len(partners))


def swap_along_x(x, strip, src, dst, relay, local_sem, send_sem, recv_sem):
    right, left, opposite = wrap(x + 1, SIDE), wrap(x - 1, SIDE), wrap(x + 2, SIDE)
    half = src.shape[-1] // 2
    low, high = pl.ds(0, half), pl.ds(half, half)

    def copy(source, target, slot, to):
        return pltpu.make_async_remote_copy(
            src_ref=source,
            dst_ref=target,
            send_sem=send_sem.at[slot],
            recv_sem=recv_sem.at[slot],
            device_id=(to, strip),
            device_id_type=MESH,
        )

    out_low = copy(src.at[opposite, :, low], relay.at[0], 0, right)
    out_high = copy(src.at[opposite, :, high], relay.at[1], 1, left)
    to_right = copy(src.at[right], dst.at[x], 2, right)
    to_left = copy(src.at[left], dst.at[x], 3, left)
    out_low.start()
    out_high.start()
    to_right.start()
    to_left.start()
    mine = pltpu.make_async_copy(src.at[x], dst.at[x], local_sem)
    mine.start()
    out_low.wait_recv()
    on_low = copy(relay.at[0], dst.at[left, :, low], 4, right)
    on_low.start()
    out_high.wait_recv()
    on_high = copy(relay.at[1], dst.at[right, :, high], 5, left)
    on_high.start()
    mine.wait()
    copy(src.at[right], dst.at[left], 2, right).wait_recv()
    copy(src.at[left], dst.at[right], 3, left).wait_recv()
    copy(relay.at[0], dst.at[opposite, :, low], 4, right).wait_recv()
    copy(relay.at[1], dst.at[opposite, :, high], 5, left).wait_recv()
    for sent in (out_low, out_high, to_right, to_left, on_low, on_high):
        sent.wait_send()


def gram_kernel(
    resid, swapped, gram, relay, part, pieces, in_y, in_z, total,
    local_sem, swap_send, swap_recv, first_send, first_recv, y_send, y_recv, z_send, z_recv,
    last_send, last_recv,
):
    x, strip, y, z, core = place()
    group = x * 2 + core

    def of_group(k):
        return (lax.div(k, 2), strip - core + lax.rem(k, 2))

    def of_y(k):
        return (x, (k * 4 + z) * 2 + core)

    def of_z(k):
        return (x, (y * 4 + k) * 2 + core)

    partners = [of_group(wrap(group + k, 8)) for k in range(1, 8)]
    partners += [of_y(wrap(y + k, 4)) for k in range(1, 4)]
    partners += [of_z(wrap(z + k, 4)) for k in range(1, 4)]
    greet(partners)
    swap_along_x(x, strip, resid, swapped, relay, local_sem, swap_send, swap_recv)

    frames = part.shape[0] * part.shape[1]
    pixels = swapped.shape[-1]
    chunk = 1024

    def add(step, so_far):
        cols = pl.ds(pl.multiple_of(step * chunk, chunk), chunk)
        block = swapped[:, :, cols].reshape(frames, chunk)
        return so_far + lax.dot_general(
            block, block, (((1,), (1,)), ((), ())), preferred_element_type=F32
        )

    partial = lax.fori_loop(0, pixels // chunk, add, jnp.zeros((frames, frames), F32))
    part[...] = partial.reshape(part.shape)

    def exchange(index, size, where, source_of, buffer, send_sem, recv_sem):
        copies = []
        for k in range(1, size):
            to = wrap(index + k, size)
            copies.append(
                pltpu.make_async_remote_copy(
                    src_ref=source_of(to),
                    dst_ref=buffer.at[index],
                    send_sem=send_sem.at[k],
                    recv_sem=recv_sem.at[k],
                    device_id=where(to),
                    device_id_type=MESH,
                )
            )
        for copy in copies:
            copy.start()
        return copies

    def arrive(index, size, where, source_of, buffer, send_sem, recv_sem, copies):
        for k in range(1, size):
            pltpu.make_async_remote_copy(
                src_ref=source_of(wrap(index + k, size)),
                dst_ref=buffer.at[wrap(index - k, size)],
                send_sem=send_sem.at[k],
                recv_sem=recv_sem.at[k],
                device_id=where(wrap(index + k, size)),
                device_id_type=MESH,
            ).wait_recv()
        for copy in copies:
            copy.wait_send()

    def added(buffer, size):
        out = buffer[0]
        for k in range(1, size):
            out = out + buffer[k]
        return out

    args = (group, 8, of_group, lambda k: part.at[k], pieces, first_send, first_recv)
    copies = exchange(*args)
    pieces[group] = part[group]
    arrive(*args, copies)
    in_y[y] = added(pieces, 8)

    args = (y, 4, of_y, lambda k: in_y.at[y], in_y, y_send, y_recv)
    arrive(*args, exchange(*args))
    in_z[z] = added(in_y, 4)

    args = (z, 4, of_z, lambda k: in_z.at[z], in_z, z_send, z_recv)
    arrive(*args, exchange(*args))
    total[group] = added(in_z, 4)

    args = (group, 8, of_group, lambda k: total.at[group], total, last_send, last_recv)
    arrive(*args, exchange(*args))
    gram[...] = total[...].reshape(gram.shape)


def gram_of(resid):
    chans, count, pixels = resid.shape
    frames = count * SIDE
    rows = frames // 8
    dma = pltpu.SemaphoreType.DMA
    return pl.pallas_call(
        gram_kernel,
        out_shape=(
            jax.ShapeDtypeStruct((SIDE, count, pixels), BF16),
            jax.ShapeDtypeStruct((frames, frames), F32),
        ),
        in_specs=in_vmem(1),
        out_specs=tuple(in_vmem(2)),
        scratch_shapes=[
            VMEM((2, count, pixels // 2), BF16),
            VMEM((8, rows, frames), F32),
            VMEM((8, rows, frames), F32),
            VMEM((4, rows, frames), F32),
            VMEM((4, rows, frames), F32),
            VMEM((8, rows, frames), F32),
            dma,
            dma((6,)), dma((6,)),
            dma((8,)), dma((8,)),
            dma((4,)), dma((4,)),
            dma((4,)), dma((4,)),
            dma((8,)), dma((8,)),
        ],
        compiler_params=pltpu.CompilerParams(
            collective_id=0, has_side_effects=True, vmem_limit_bytes=40 << 20
        ),
        name="gram",
    )(resid)


def exact(left, right, dims):
    return lax.dot_general(
        left, right, (dims, ((), ())), precision=lax.Precision.HIGHEST, preferred_element_type=F32
    )


def lower_solve(square, sides):
    size = square.shape[0]
    blocks = size // 8
    sub = lax.broadcasted_iota(jnp.int32, (8, 128), 0)
    tiles = [square[8 * i : 8 * i + 8, :] for i in range(blocks)]
    hands = [[side[8 * i : 8 * i + 8, :] for i in range(blocks)] for side in sides]
    solved = [[] for _ in sides]
    for b in range(blocks):
        cols = [
            [
                jnp.broadcast_to(tiles[i][:, 8 * b + t : 8 * b + t + 1], (8, 128))
                if i >= b
                else None
                for i in range(blocks)
            ]
            for t in range(8)
        ]
        pivot = [
            [
                jnp.broadcast_to(cols[t][b][u : u + 1, :], (8, 128)) if u >= t else None
                for u in range(8)
            ]
            for t in range(8)
        ]
        rate = []
        low = [[None] * 8 for _ in range(8)]
        for t in range(8):
            rate.append(lax.rsqrt(pivot[t][t]))
            for u in range(t + 1, 8):
                low[u][t] = pivot[t][u] * rate[t]
            for u in range(t + 1, 8):
                for v in range(u, 8):
                    pivot[u][v] = pivot[u][v] - low[u][t] * low[v][t]

        def reduced(rows):
            done = []
            for t in range(8):
                value = rows[t]
                for s in range(t):
                    value = value - done[s] * low[t][s][:, : value.shape[1]]
                done.append(value * rate[t][:, : value.shape[1]])
            return done

        below = {i: reduced([cols[t][i] for t in range(8)]) for i in range(b + 1, blocks)}
        if b + 1 < blocks:
            across = reduced(
                [jnp.broadcast_to(tiles[b][t : t + 1, :], (8, size)) for t in range(8)]
            )
            for i in range(b + 1, blocks):
                for t in range(8):
                    tiles[i] = tiles[i] - below[i][t][:, :size] * across[t]
        for hand, out in zip(hands, solved):
            rows = reduced([jnp.broadcast_to(hand[b][t : t + 1, :], (8, 128)) for t in range(8)])
            tile = rows[0]
            for t in range(1, 8):
                tile = jnp.where(sub == t, rows[t], tile)
            out.append(tile)
            for i in range(b + 1, blocks):
                for t in range(8):
                    hand[i] = hand[i] - below[i][t] * rows[t]
    return [jnp.concatenate(out, axis=0) for out in solved]


def mixing_kernel(nval, gram_ref, sketch_ref, mixing_ref, gram_sc, basis_sc):
    gram_sc[...] = gram_ref[...] * (1.0 / nval)
    basis_sc[...] = sketch_ref[...]

    def turn(step, carry):
        basis = basis_sc[...]
        image = exact(basis, gram_sc[...], ((1,), (1,)))
        square = exact(basis, image, ((1,), (1,)))
        basis_sc[...] = lower_solve(square, [image])[0]
        return carry

    lax.fori_loop(0, POWER, turn, 0)
    basis = basis_sc[...]
    image = exact(basis, gram_sc[...], ((1,), (0,)))
    square = exact(basis, image, ((1,), (1,)))
    left, right = lower_solve(square, [basis, image])
    mixing_ref[...] = exact(right, left, ((0,), (0,))).astype(BF16)


def mixing_of(gram, sketch, nval):
    frames, rank = sketch.shape
    return pl.pallas_call(
        functools.partial(mixing_kernel, nval),
        out_shape=jax.ShapeDtypeStruct((frames, frames), BF16),
        in_specs=in_vmem(2),
        out_specs=in_vmem(1)[0],
        scratch_shapes=[VMEM((frames, frames), F32), VMEM((rank, frames), F32)],
        name="mixing",
    )(gram, sketch.T)


def back_kernel(
    swapped, weights, frames, valid, back, above, below,
    made, relay, top, bottom, local_sem, swap_send, swap_recv, halo_send, halo_recv,
):
    x, strip, _, _, _ = place()
    strips = lax.axis_size("pix")
    up, down = wrap(strip - 1, strips), wrap(strip + 1, strips)
    greet([(wrap(x + 1, SIDE), strip), (wrap(x - 1, SIDE), strip), (x, up), (x, down)])
    side, count, pixels = swapped.shape
    chunk = 1024
    mix = weights[...]

    def multiply(step, carry):
        cols = pl.ds(pl.multiple_of(step * chunk, chunk), chunk)
        block = swapped[:, :, cols].reshape(side * count, chunk)
        out = jnp.dot(mix, block, preferred_element_type=F32)
        made[:, :, cols] = out.astype(BF16).reshape(side, count, chunk)
        return carry

    lax.fori_loop(0, pixels // chunk, multiply, 0)
    swap_along_x(x, strip, made, back, relay, local_sem, swap_send, swap_recv)
    width = top.shape[-1]
    for chan in range(side):
        for target, start in ((top, 0), (bottom, pixels - width)):
            cols = slice(start, start + width)
            source = frames[chan, :, cols].astype(F32) - back[chan, :, cols].astype(F32)
            if chan == side - 1:
                source = source * valid[:, cols].astype(F32)
            target[chan] = source.astype(BF16)
    copies = []
    for k, (source, target, to) in enumerate(((top, below, up), (bottom, above, down))):
        copies.append(
            pltpu.make_async_remote_copy(
                src_ref=source,
                dst_ref=target,
                send_sem=halo_send.at[k],
                recv_sem=halo_recv.at[k],
                device_id=(x, to),
                device_id_type=MESH,
            )
        )
    for copy in copies:
        copy.start()
    for copy in copies:
        copy.wait()


def back_of(swapped, weights, frames, valid, cols):
    side, count, pixels = swapped.shape
    dma = pltpu.SemaphoreType.DMA
    halo = (side, count, NSWEEP * cols)
    return pl.pallas_call(
        back_kernel,
        out_shape=(
            jax.ShapeDtypeStruct(swapped.shape, BF16),
            jax.ShapeDtypeStruct(halo, BF16),
            jax.ShapeDtypeStruct(halo, BF16),
        ),
        in_specs=in_vmem(4),
        out_specs=tuple(in_vmem(3)),
        scratch_shapes=[
            VMEM(swapped.shape, BF16),
            VMEM((2, count, pixels // 2), BF16),
            VMEM(halo, BF16),
            VMEM(halo, BF16),
            dma,
            dma((6,)), dma((6,)),
            dma((2,)), dma((2,)),
        ],
        compiler_params=pltpu.CompilerParams(
            collective_id=1, has_side_effects=True, vmem_limit_bytes=40 << 20
        ),
        name="back",
    )(swapped, weights, frames, valid)


def tv_kernel(strips, strip_ref, lam_ref, frames, back, valid, above, below, out, source, first, second):
    chan = pl.program_id(0)
    last = pl.num_programs(0) - 1
    lam = lam_ref[chan]
    inverse = 1.0 / lam
    strip = strip_ref[0]
    halo = NSWEEP
    span, lines, cols = source.shape
    rows = span - 2 * halo
    tiles = cols // 128
    lane = lax.broadcasted_iota(jnp.int32, (lines, 128), 1)
    open_above = jnp.where(strip > 0, F32(1.0), F32(0.0))
    open_below = jnp.where(strip < strips - 1, F32(1.0), F32(0.0))

    def tile(ref, r):
        return [ref[r, :, 128 * j : 128 * j + 128] for j in range(tiles)]

    def put(ref, r, values):
        for j in range(tiles):
            ref[r, :, 128 * j : 128 * j + 128] = values[j]

    for r in range(halo):
        source[r] = above[0, :, r * cols : (r + 1) * cols].astype(F32) * 0.125
        source[halo + rows + r] = below[0, :, r * cols : (r + 1) * cols].astype(F32) * 0.125
    for r in range(rows):
        where = slice(r * cols, (r + 1) * cols)
        ok = jnp.where(chan == last, valid[:, where].astype(F32), 1.0)
        source[halo + r] = (frames[0, :, where].astype(F32) - back[0, :, where].astype(F32)) * (ok * 0.125)

    def before(values):
        turned = [pltpu.roll(v, 1, 1) for v in values]
        return [jnp.where(lane == 0, turned[j - 1] if j else 0.0, turned[j]) for j in range(tiles)]

    def after(values):
        turned = [pltpu.roll(v, 127, 1) for v in values]
        return [jnp.where(lane == 127, turned[j + 1] if j + 1 < tiles else values[j], turned[j]) for j in range(tiles)]

    def image(r, up, here, beside, scale=0.125):
        left = before(beside)
        return [s - scale * ((h - u) + (b - l)) for s, u, h, b, l in zip(tile(source, r), up, here, beside, left)]

    def update(r, smooth, under, here, beside):
        right = after(smooth)
        news = []
        for j in range(tiles):
            down = under[j] - smooth[j]
            if r == halo - 1:
                down = down * open_above
            if r == halo + rows - 1:
                down = down * open_below
            across = right[j] - smooth[j]
            square = jnp.maximum(down * down + across * across, 1e-37)
            rate = 1.0 / (1.0 + inverse * (square * lax.rsqrt(square)))
            a = -down if here is None else here[j] - down
            b = -across if beside is None else beside[j] - across
            news.append((a * rate, b * rate))
        put(first, r, [n[0] for n in news])
        put(second, r, [n[1] for n in news])

    smooth = tile(source, 0)
    for r in range(span - 1):
        under = tile(source, r + 1)
        update(r, smooth, under, None, None)
        smooth = under
    for sweep in range(1, NSWEEP):
        here, beside = tile(first, sweep), tile(second, sweep)
        smooth = image(sweep, tile(first, sweep - 1), here, beside)
        for r in range(sweep, span - 1 - sweep):
            next_here, next_beside = tile(first, r + 1), tile(second, r + 1)
            under = image(r + 1, here, next_here, next_beside)
            update(r, smooth, under, here, beside)
            smooth, here, beside = under, next_here, next_beside
    for r in range(rows):
        i = halo + r
        values = image(i, tile(first, i - 1), tile(first, i), tile(second, i))
        for j in range(tiles):
            out[0, :, r * cols + 128 * j : r * cols + 128 * j + 128] = (values[j] * 8.0).astype(BF16)


def foreground_of(frames, back, valid, above, below, lam, strip, strips, cols):
    chans, count, pixels = frames.shape
    lines = 32
    rows = pixels // cols
    span = rows + 2 * NSWEEP
    whole = pl.BlockSpec((1, lines, pixels), lambda c, f, *_: (c, f, 0))
    edge = pl.BlockSpec((1, lines, NSWEEP * cols), lambda c, f, *_: (c, f, 0))
    scalar = pl.BlockSpec(memory_space=pltpu.SMEM)
    return pl.pallas_call(
        functools.partial(tv_kernel, strips),
        grid=(chans, count // lines),
        out_shape=jax.ShapeDtypeStruct(frames.shape, BF16),
        in_specs=[
            scalar,
            scalar,
            whole,
            whole,
            pl.BlockSpec((lines, pixels), lambda c, f: (f, 0)),
            edge,
            edge,
        ],
        out_specs=whole,
        scratch_shapes=[VMEM((span, lines, cols), F32)] * 3,
        compiler_params=pltpu.CompilerParams(vmem_limit_bytes=40 << 20),
        name="tv",
    )(strip, lam, frames, back, valid, above, below)


def local(frames, prev_fg, depth_valid, sketch, tv_weight):
    count, chans, rows, cols = frames.shape
    strips = lax.axis_size("pix")
    nval = chans * rows * strips * cols
    chan_ids = lax.broadcasted_iota(jnp.int32, (1, chans, 1, 1), 1)
    depth_ok = depth_valid[:, None, :, :].astype(F32)
    valid = jnp.where(chan_ids == chans - 1, depth_ok, F32(1.0))
    resid = ((frames.astype(F32) - prev_fg.astype(F32)) * valid).astype(BF16)

    def flat(value):
        return value.transpose(1, 0, 2, 3).reshape(chans, count, rows * cols)

    resid, frames = flat(resid), flat(frames)
    ok = depth_valid.astype(BF16).reshape(count, rows * cols)
    swapped, gram = gram_of(resid)
    weights = mixing_of(gram, sketch, nval)
    back, above, below = back_of(swapped, weights, frames, ok, cols)
    strip = lax.axis_index("pix").reshape(1)
    fore = foreground_of(frames, back, ok, above, below, tv_weight, strip, strips, cols)

    def unflat(value):
        return value.reshape(chans, count, rows, cols).transpose(1, 0, 2, 3)

    return unflat(back), unflat(fore)


def solution(mesh):
    placed = (
        P("frame", None, "pix", None),
        P("frame", None, "pix", None),
        P("frame", "pix", None),
        P(),
        P(),
    )
    return jax.shard_map(
        local,
        mesh=mesh,
        in_specs=placed,
        out_specs=(P("frame", None, "pix", None), P("frame", None, "pix", None)),
        check_vma=False,
    )
```

```python
import functools

import jax
import jax.numpy as jnp
from jax import lax
from jax.experimental import pallas as pl
from jax.experimental.pallas import tpu as pltpu
from jax.sharding import PartitionSpec as P

POWER = 3
NSWEEP = 5
STEP_SIZE = 0.125
MESH = pl.DeviceIdType.MESH
VMEM = pltpu.VMEM
SIDE = 4
BF16 = jnp.bfloat16
F32 = jnp.float32


def in_vmem(count):
    return [pl.BlockSpec(memory_space=pltpu.VMEM)] * count


def wrap(value, size):
    return lax.rem(value + size, size)


def place():
    x = lax.axis_index("frame")
    strip = lax.axis_index("pix")
    return x, strip, lax.div(strip, 8), lax.rem(lax.div(strip, 2), 4), lax.rem(strip, 2)


def greet(partners):
    barrier = pltpu.get_barrier_semaphore()
    for partner in partners:
        pl.semaphore_signal(barrier, inc=1, device_id=partner, device_id_type=MESH)
    pl.semaphore_wait(barrier, len(partners))


def send_along_x(x, strip, src, dst, send_sem, recv_sem, offset):
    to = wrap(x + offset, SIDE)
    return pltpu.make_async_remote_copy(
        src_ref=src.at[to],
        dst_ref=dst.at[x],
        send_sem=send_sem.at[offset],
        recv_sem=recv_sem.at[offset],
        device_id=(to, strip),
        device_id_type=MESH,
    )


def taken_along_x(x, strip, src, dst, send_sem, recv_sem, offset):
    origin = wrap(x - offset, SIDE)
    return pltpu.make_async_remote_copy(
        src_ref=src.at[origin],
        dst_ref=dst.at[origin],
        send_sem=send_sem.at[offset],
        recv_sem=recv_sem.at[offset],
        device_id=(origin, strip),
        device_id_type=MESH,
    )


ORDER = (2, 1, 3)


def lay(lines, start, value):
    count, rows, cols = value.shape
    value = value.reshape(count * rows, cols)
    for j in range(lines.shape[0]):
        lines[j, start * rows : (start + count) * rows, :] = value[:, 128 * j : 128 * j + 128]


def turned(lines, write, rows):
    tiles, size, _ = lines.shape
    for r in range(rows):
        for j in range(tiles):
            start = (r * tiles + j) * 128
            value = lines.at[j][pl.ds(r, size // rows, stride=rows), :]
            write(slice(start, start + 128), value)


def gram_kernel(
    frames_hbm, prev_hbm, depth_hbm, swapped, gram, flat_frames, flat_valid,
    frames, prev, depth, flat, lines, part, pieces, in_y, in_z, total,
    load_sem, swap_send, swap_recv, first_send, first_recv, y_send, y_recv, z_send, z_recv,
    last_send, last_recv,
):
    x, strip, y, z, core = place()
    group = x * 2 + core
    count, chans, rows, cols = frames.shape
    channels = [wrap(x + offset, SIDE) for offset in ORDER + (0,)]
    loads = []
    first = pltpu.make_async_copy(depth_hbm, depth, load_sem.at[2 * chans])
    first.start()
    for k, chan in enumerate(channels):
        pair = [
            pltpu.make_async_copy(hbm.at[:, chan], vmem.at[:, chan], load_sem.at[2 * k + j])
            for j, (hbm, vmem) in enumerate(((frames_hbm, frames), (prev_hbm, prev)))
        ]
        for copy in pair:
            copy.start()
        loads.append(pair)

    def of_group(k):
        return (lax.div(k, 2), strip - core + lax.rem(k, 2))

    def of_y(k):
        return (x, (k * 4 + z) * 2 + core)

    def of_z(k):
        return (x, (y * 4 + k) * 2 + core)

    partners = [of_group(wrap(group + k, 8)) for k in range(1, 8)]
    partners += [of_y(wrap(y + k, 4)) for k in range(1, 4)]
    partners += [of_z(wrap(z + k, 4)) for k in range(1, 4)]
    barrier = pltpu.get_barrier_semaphore()
    for partner in partners:
        pl.semaphore_signal(barrier, inc=1, device_id=partner, device_id_type=MESH)

    def residual(chan, write):
        for f in range(0, count, 8):
            ok = jnp.where(chan == chans - 1, depth[f : f + 8].astype(F32), 1.0)
            value = (
                frames[f : f + 8, chan].astype(F32) - prev[f : f + 8, chan].astype(F32)
            ) * ok
            lay(lines, f, value)
        turned(lines, write, rows)

    args = (x, strip, flat, swapped, swap_send, swap_recv)
    sends = []
    first.wait()
    for k, offset in enumerate(ORDER):
        for copy in loads[k]:
            copy.wait()

        def write(where, value, chan=channels[k]):
            flat[chan, :, where] = value.astype(BF16)

        residual(channels[k], write)
        if k == 0:
            pl.semaphore_wait(barrier, len(partners))
        sends.append(send_along_x(*args, offset))
        sends[-1].start()
    for copy in loads[-1]:
        copy.wait()

    def write_own(where, value):
        swapped[x, :, where] = value.astype(BF16)

    residual(x, write_own)

    def write_valid(where, value):
        flat_valid[:, where] = value.astype(BF16)

    lay(lines, 0, depth[...].astype(F32))
    turned(lines, write_valid, rows)
    for chan in range(chans):

        def write_frames(where, value):
            flat_frames[chan, :, where] = value.astype(BF16)

        for f in range(0, count, 8):
            lay(lines, f, frames[f : f + 8, chan].astype(F32))
        turned(lines, write_frames, rows)
    for offset in ORDER:
        taken_along_x(*args, offset).wait_recv()
    for copy in sends:
        copy.wait_send()

    every = part.shape[0] * part.shape[1]
    pixels = swapped.shape[-1]
    chunk = 1024

    def add(step, so_far):
        cols = pl.ds(pl.multiple_of(step * chunk, chunk), chunk)
        block = swapped[:, :, cols].reshape(every, chunk)
        return so_far + lax.dot_general(
            block, block, (((1,), (1,)), ((), ())), preferred_element_type=F32
        )

    partial = lax.fori_loop(0, pixels // chunk, add, jnp.zeros((every, every), F32))
    part[...] = partial.reshape(part.shape)

    def exchange(index, size, where, source_of, buffer, send_sem, recv_sem):
        copies = []
        for k in range(1, size):
            to = wrap(index + k, size)
            copies.append(
                pltpu.make_async_remote_copy(
                    src_ref=source_of(to),
                    dst_ref=buffer.at[index],
                    send_sem=send_sem.at[k],
                    recv_sem=recv_sem.at[k],
                    device_id=where(to),
                    device_id_type=MESH,
                )
            )
        for copy in copies:
            copy.start()
        return copies

    def arrive(index, size, where, source_of, buffer, send_sem, recv_sem, copies):
        for k in range(1, size):
            pltpu.make_async_remote_copy(
                src_ref=source_of(wrap(index + k, size)),
                dst_ref=buffer.at[wrap(index - k, size)],
                send_sem=send_sem.at[k],
                recv_sem=recv_sem.at[k],
                device_id=where(wrap(index + k, size)),
                device_id_type=MESH,
            ).wait_recv()
        for copy in copies:
            copy.wait_send()

    def added(buffer, size):
        out = buffer[0]
        for k in range(1, size):
            out = out + buffer[k]
        return out

    args = (group, 8, of_group, lambda k: part.at[k], pieces, first_send, first_recv)
    copies = exchange(*args)
    pieces[group] = part[group]
    arrive(*args, copies)
    in_y[y] = added(pieces, 8)

    args = (y, 4, of_y, lambda k: in_y.at[y], in_y, y_send, y_recv)
    arrive(*args, exchange(*args))
    in_z[z] = added(in_y, 4)

    args = (z, 4, of_z, lambda k: in_z.at[z], in_z, z_send, z_recv)
    arrive(*args, exchange(*args))
    total[group] = added(in_z, 4)

    args = (group, 8, of_group, lambda k: total.at[group], total, last_send, last_recv)
    arrive(*args, exchange(*args))
    gram[...] = total[...].reshape(gram.shape)


def gram_of(frames, prev_fg, depth_valid):
    count, chans, rows, cols = frames.shape
    pixels = rows * cols
    every = count * SIDE
    piece = every // 8
    dma = pltpu.SemaphoreType.DMA
    return pl.pallas_call(
        gram_kernel,
        out_shape=(
            jax.ShapeDtypeStruct((SIDE, count, pixels), BF16),
            jax.ShapeDtypeStruct((every, every), F32),
            jax.ShapeDtypeStruct((chans, count, pixels), BF16),
            jax.ShapeDtypeStruct((count, pixels), BF16),
        ),
        in_specs=[pl.BlockSpec(memory_space=pltpu.HBM)] * 3,
        out_specs=tuple(in_vmem(4)),
        scratch_shapes=[
            VMEM(frames.shape, BF16),
            VMEM(frames.shape, BF16),
            VMEM(depth_valid.shape, jnp.int32),
            VMEM((chans, count, pixels), BF16),
            VMEM((cols // 128, count * rows, 128), F32),
            VMEM((8, piece, every), F32),
            VMEM((8, piece, every), F32),
            VMEM((4, piece, every), F32),
            VMEM((4, piece, every), F32),
            VMEM((8, piece, every), F32),
            dma((2 * chans + 1,)),
            dma((4,)), dma((4,)),
            dma((8,)), dma((8,)),
            dma((4,)), dma((4,)),
            dma((4,)), dma((4,)),
            dma((8,)), dma((8,)),
        ],
        compiler_params=pltpu.CompilerParams(
            collective_id=0, has_side_effects=True, vmem_limit_bytes=48 << 20
        ),
        name="gram",
    )(frames, prev_fg, depth_valid)


def exact(left, right, dims):
    return lax.dot_general(
        left, right, (dims, ((), ())), precision=lax.Precision.HIGHEST, preferred_element_type=F32
    )


def lower_solve(square, sides):
    size = square.shape[0]
    blocks = size // 8
    sub = lax.broadcasted_iota(jnp.int32, (8, 128), 0)
    tiles = [square[8 * i : 8 * i + 8, :] for i in range(blocks)]
    hands = [[side[8 * i : 8 * i + 8, :] for i in range(blocks)] for side in sides]
    solved = [[] for _ in sides]
    for b in range(blocks):
        cols = [
            [
                jnp.broadcast_to(tiles[i][:, 8 * b + t : 8 * b + t + 1], (8, 128))
                if i >= b
                else None
                for i in range(blocks)
            ]
            for t in range(8)
        ]
        pivot = [
            [
                jnp.broadcast_to(cols[t][b][u : u + 1, :], (8, 128)) if u >= t else None
                for u in range(8)
            ]
            for t in range(8)
        ]
        rate = []
        low = [[None] * 8 for _ in range(8)]
        for t in range(8):
            rate.append(lax.rsqrt(pivot[t][t]))
            for u in range(t + 1, 8):
                low[u][t] = pivot[t][u] * rate[t]
            for u in range(t + 1, 8):
                for v in range(u, 8):
                    pivot[u][v] = pivot[u][v] - low[u][t] * low[v][t]

        def reduced(rows):
            done = []
            for t in range(8):
                value = rows[t]
                for s in range(t):
                    value = value - done[s] * low[t][s][:, : value.shape[1]]
                done.append(value * rate[t][:, : value.shape[1]])
            return done

        below = {i: reduced([cols[t][i] for t in range(8)]) for i in range(b + 1, blocks)}
        if b + 1 < blocks:
            across = reduced(
                [jnp.broadcast_to(tiles[b][t : t + 1, :], (8, size)) for t in range(8)]
            )
            for i in range(b + 1, blocks):
                for t in range(8):
                    tiles[i] = tiles[i] - below[i][t][:, :size] * across[t]
        for hand, out in zip(hands, solved):
            rows = reduced([jnp.broadcast_to(hand[b][t : t + 1, :], (8, 128)) for t in range(8)])
            tile = rows[0]
            for t in range(1, 8):
                tile = jnp.where(sub == t, rows[t], tile)
            out.append(tile)
            for i in range(b + 1, blocks):
                for t in range(8):
                    hand[i] = hand[i] - below[i][t] * rows[t]
    return [jnp.concatenate(out, axis=0) for out in solved]


def mixing_kernel(nval, gram_ref, sketch_ref, mixing_ref, gram_sc, basis_sc):
    gram_sc[...] = gram_ref[...] * (1.0 / nval)
    basis_sc[...] = sketch_ref[...]

    def turn(step, carry):
        basis = basis_sc[...]
        image = exact(basis, gram_sc[...], ((1,), (1,)))
        square = exact(basis, image, ((1,), (1,)))
        basis_sc[...] = lower_solve(square, [image])[0]
        return carry

    lax.fori_loop(0, POWER, turn, 0)
    basis = basis_sc[...]
    image = exact(basis, gram_sc[...], ((1,), (0,)))
    square = exact(basis, image, ((1,), (1,)))
    left, right = lower_solve(square, [basis, image])
    mixing_ref[...] = exact(right, left, ((0,), (0,))).astype(BF16)


def mixing_of(gram, sketch, nval):
    frames, rank = sketch.shape
    return pl.pallas_call(
        functools.partial(mixing_kernel, nval),
        out_shape=jax.ShapeDtypeStruct((frames, frames), BF16),
        in_specs=in_vmem(2),
        out_specs=in_vmem(1)[0],
        scratch_shapes=[VMEM((frames, frames), F32), VMEM((rank, frames), F32)],
        compiler_params=pltpu.CompilerParams(vmem_limit_bytes=4 << 20),
        name="mixing",
    )(gram, sketch.T)


def smooth_channel(
    strips, strip, chan, offset, lam_ref, frames, back, valid, above, below, out,
    source, first, second, between,
):
    inverse = 1.0 / lam_ref[chan]
    last = frames.shape[0] - 1
    halo = NSWEEP
    span, lines, cols = source.shape
    rows = span - 2 * halo
    tiles = cols // 128
    lane = lax.broadcasted_iota(jnp.int32, (lines, 128), 1)
    open_above = jnp.where(strip > 0, F32(1.0), F32(0.0))
    open_below = jnp.where(strip < strips - 1, F32(1.0), F32(0.0))

    def tile(ref, r):
        return [ref[r, :, 128 * j : 128 * j + 128] for j in range(tiles)]

    def put(ref, r, values):
        for j in range(tiles):
            ref[r, :, 128 * j : 128 * j + 128] = values[j]

    for r in range(halo):
        source[r] = above[offset, :, r * cols : (r + 1) * cols].astype(F32) * 0.125
        source[halo + rows + r] = below[offset, :, r * cols : (r + 1) * cols].astype(F32) * 0.125
    for r in range(rows):
        where = slice(r * cols, (r + 1) * cols)
        ok = jnp.where(chan == last, valid[:, where].astype(F32), 1.0)
        source[halo + r] = (frames[chan, :, where].astype(F32) - back[chan, :, where].astype(F32)) * (ok * 0.125)

    def before(values):
        turned = [pltpu.roll(v, 1, 1) for v in values]
        return [jnp.where(lane == 0, turned[j - 1] if j else 0.0, turned[j]) for j in range(tiles)]

    def after(values):
        turned = [pltpu.roll(v, 127, 1) for v in values]
        return [jnp.where(lane == 127, turned[j + 1] if j + 1 < tiles else values[j], turned[j]) for j in range(tiles)]

    def image(r, up, here, beside, scale=0.125):
        left = before(beside)
        return [s - scale * ((h - u) + (b - l)) for s, u, h, b, l in zip(tile(source, r), up, here, beside, left)]

    def update(r, smooth, under, here, beside):
        right = after(smooth)
        news = []
        for j in range(tiles):
            down = under[j] - smooth[j]
            if r == halo - 1:
                down = down * open_above
            if r == halo + rows - 1:
                down = down * open_below
            across = right[j] - smooth[j]
            square = jnp.maximum(down * down + across * across, 1e-37)
            rate = 1.0 / (1.0 + inverse * (square * lax.rsqrt(square)))
            a = -down if here is None else here[j] - down
            b = -across if beside is None else beside[j] - across
            news.append((a * rate, b * rate))
        put(first, r, [n[0] for n in news])
        put(second, r, [n[1] for n in news])

    smooth = tile(source, 0)
    for r in range(span - 1):
        under = tile(source, r + 1)
        update(r, smooth, under, None, None)
        smooth = under
    for sweep in range(1, NSWEEP):
        if sweep == 3:
            between()
        here, beside = tile(first, sweep), tile(second, sweep)
        smooth = image(sweep, tile(first, sweep - 1), here, beside)
        for r in range(sweep, span - 1 - sweep):
            next_here, next_beside = tile(first, r + 1), tile(second, r + 1)
            under = image(r + 1, here, next_here, next_beside)
            update(r, smooth, under, here, beside)
            smooth, here, beside = under, next_here, next_beside
    for r in range(rows):
        i = halo + r
        values = image(i, tile(first, i - 1), tile(first, i), tile(second, i))
        for j in range(tiles):
            out[chan, :, r * cols + 128 * j : r * cols + 128 * j + 128] = (values[j] * 8.0).astype(BF16)


def finish_kernel(
    lam_ref, swapped, weights, frames, valid, back, fore,
    made, top, bottom, above, below, source, first, second,
    local_sem, swap_send, swap_recv, halo_send, halo_recv,
):
    x, strip, _, _, _ = place()
    strips = lax.axis_size("pix")
    up, down = wrap(strip - 1, strips), wrap(strip + 1, strips)
    partners = [(wrap(x + k, SIDE), strip) for k in ORDER] + [(x, up), (x, down)]
    barrier = pltpu.get_barrier_semaphore()
    for partner in partners:
        pl.semaphore_signal(barrier, inc=1, device_id=partner, device_id_type=MESH)
    side, count, pixels = swapped.shape
    width = top.shape[-1]
    cols = source.shape[-1]
    parts = ((0, width), (pixels - width, width), (width, pixels - 2 * width))
    mix = weights[...]

    def multiply(part):
        start, size = parts[part]
        for at in range(start, start + size, 512):
            where = slice(at, at + 512)
            block = swapped[:, :, where].reshape(side * count, 512)
            out = jnp.dot(mix, block, preferred_element_type=F32)
            made[:, :, where] = out.astype(BF16).reshape(side, count, 512)

    def send(offset, part):
        to = wrap(x + offset, SIDE)
        where = pl.ds(*parts[part])
        return pltpu.make_async_remote_copy(
            src_ref=made.at[to, :, where],
            dst_ref=back.at[x, :, where],
            send_sem=swap_send.at[offset, part],
            recv_sem=swap_recv.at[offset, part],
            device_id=(to, strip),
            device_id_type=MESH,
        )

    def taken(offset, part):
        origin = wrap(x - offset, SIDE)
        where = pl.ds(*parts[part])
        return pltpu.make_async_remote_copy(
            src_ref=made.at[origin, :, where],
            dst_ref=back.at[origin, :, where],
            send_sem=swap_send.at[offset, part],
            recv_sem=swap_recv.at[offset, part],
            device_id=(origin, strip),
            device_id_type=MESH,
        )

    def halo(offset, way):
        outgoing, incoming, to = ((top, below, up), (bottom, above, down))[way]
        return pltpu.make_async_remote_copy(
            src_ref=outgoing.at[offset],
            dst_ref=incoming.at[offset],
            send_sem=halo_send.at[offset, way],
            recv_sem=halo_recv.at[offset, way],
            device_id=(x, to),
            device_id_type=MESH,
        )

    def forward(offset):
        chan = wrap(x - offset, SIDE)
        if offset:
            taken(offset, 0).wait_recv()
            taken(offset, 1).wait_recv()
        for way, target in ((0, top), (1, bottom)):
            where = slice(parts[way][0], parts[way][0] + width)
            held = back if offset else made
            edge = frames[chan, :, where].astype(F32) - held[chan, :, where].astype(F32)
            ok = jnp.where(chan == side - 1, valid[:, where].astype(F32), 1.0)
            target[offset] = (edge * ok).astype(BF16)
        for way in range(2):
            halo(offset, way).start()

    multiply(0)
    multiply(1)
    pl.semaphore_wait(barrier, len(partners))
    forward(0)
    for offset in (1, 3):
        for part in range(2):
            send(offset, part).start()
    multiply(2)
    for offset in (1, 3):
        send(offset, 2).start()
    for part in (0, 1, 2):
        send(2, part).start()
    mine = pltpu.make_async_copy(made.at[x], back.at[x], local_sem)
    mine.start()
    mine.wait()

    def group(k, carry):
        offset = k + jnp.where(k == 2, 1, 0) - jnp.where(k == 3, 1, 0)

        @pl.when(k > 0)
        def _():
            taken(offset, 2).wait_recv()

        for way in range(2):
            halo(offset, way).wait_recv()

        def between():
            @pl.when(k == 0)
            def _():
                forward(1)
                forward(3)

            @pl.when(k == 1)
            def _():
                forward(2)

        smooth_channel(
            strips, strip, wrap(x - offset, SIDE), offset, lam_ref,
            frames, back, valid, above, below, fore, source, first, second, between,
        )
        return carry

    lax.fori_loop(0, SIDE, group, 0)
    for offset in ORDER:
        for part in range(3):
            send(offset, part).wait_send()
    for offset in range(SIDE):
        for way in range(2):
            halo(offset, way).wait_send()


def finish_of(swapped, weights, frames, valid, lam, cols):
    side, count, pixels = swapped.shape
    dma = pltpu.SemaphoreType.DMA
    edge = (side, count, NSWEEP * cols)
    field = (pixels // cols + 2 * NSWEEP, count, cols)
    return pl.pallas_call(
        finish_kernel,
        out_shape=(
            jax.ShapeDtypeStruct(swapped.shape, BF16),
            jax.ShapeDtypeStruct(swapped.shape, BF16),
        ),
        in_specs=[pl.BlockSpec(memory_space=pltpu.SMEM)] + in_vmem(4),
        out_specs=tuple(in_vmem(2)),
        scratch_shapes=[
            VMEM(swapped.shape, BF16),
            VMEM(edge, BF16),
            VMEM(edge, BF16),
            VMEM(edge, BF16),
            VMEM(edge, BF16),
            VMEM(field, F32),
            VMEM(field, F32),
            VMEM(field, F32),
            dma,
            dma((4, 3)), dma((4, 3)),
            dma((4, 2)), dma((4, 2)),
        ],
        compiler_params=pltpu.CompilerParams(
            collective_id=1, has_side_effects=True, vmem_limit_bytes=32 << 20
        ),
        name="finish",
    )(lam, swapped, weights, frames, valid)


def local(frames, prev_fg, depth_valid, sketch, tv_weight):
    count, chans, rows, cols = frames.shape
    strips = lax.axis_size("pix")
    nval = chans * rows * strips * cols
    swapped, gram, frames, ok = gram_of(frames, prev_fg, depth_valid)
    weights = mixing_of(gram, sketch, nval)
    back, fore = finish_of(swapped, weights, frames, ok, tv_weight, cols)

    def unflat(value):
        return value.reshape(chans, count, rows, cols).transpose(1, 0, 2, 3)

    return unflat(back), unflat(fore)


def solution(mesh):
    placed = (
        P("frame", None, "pix", None),
        P("frame", None, "pix", None),
        P("frame", "pix", None),
        P(),
        P(),
    )
    return jax.shard_map(
        local,
        mesh=mesh,
        in_specs=placed,
        out_specs=(P("frame", None, "pix", None), P("frame", None, "pix", None)),
        check_vma=False,
    )
```

```python
import functools

import jax
import jax.numpy as jnp
from jax import lax
from jax.experimental import pallas as pl
from jax.experimental.pallas import tpu as pltpu
from jax.sharding import PartitionSpec as P

POWER = 3
NSWEEP = 5
STEP_SIZE = 0.125
MESH = pl.DeviceIdType.MESH
VMEM = pltpu.VMEM
SIDE = 4
BF16 = jnp.bfloat16
F32 = jnp.float32


def in_vmem(count):
    return [pl.BlockSpec(memory_space=pltpu.VMEM)] * count


def wrap(value, size):
    return lax.rem(value + size, size)


def place():
    x = lax.axis_index("frame")
    strip = lax.axis_index("pix")
    return x, strip, lax.div(strip, 8), lax.rem(lax.div(strip, 2), 4), lax.rem(strip, 2)


def send_along_x(x, strip, src, dst, send_sem, recv_sem, offset, part, where):
    to = wrap(x + offset, SIDE)
    return pltpu.make_async_remote_copy(
        src_ref=src.at[to, :, where],
        dst_ref=dst.at[x, :, where],
        send_sem=send_sem.at[offset, part],
        recv_sem=recv_sem.at[offset, part],
        device_id=(to, strip),
        device_id_type=MESH,
    )


def taken_along_x(x, strip, src, dst, send_sem, recv_sem, offset, part, where):
    origin = wrap(x - offset, SIDE)
    return pltpu.make_async_remote_copy(
        src_ref=src.at[origin, :, where],
        dst_ref=dst.at[origin, :, where],
        send_sem=send_sem.at[offset, part],
        recv_sem=recv_sem.at[offset, part],
        device_id=(origin, strip),
        device_id_type=MESH,
    )


ORDER = (2, 1, 3)


def lay(lines, start, value):
    count, rows, cols = value.shape
    value = value.reshape(count * rows, cols)
    for j in range(lines.shape[0]):
        lines[j, start * rows : (start + count) * rows, :] = value[:, 128 * j : 128 * j + 128]


def turned(lines, write, rows):
    tiles, size, _ = lines.shape
    for r in range(rows):
        for j in range(tiles):
            start = (r * tiles + j) * 128
            value = lines.at[j][pl.ds(r, size // rows, stride=rows), :]
            write(slice(start, start + 128), value)


def gram_stage(
    frames_hbm, prev_hbm, depth_hbm, swapped, flat_frames, flat_valid, frames, prev, depth, flat, lines, part, pieces, in_y, in_z, total,
    load_sem, swap_send, swap_recv, first_send, first_recv, y_send, y_recv, z_send, z_recv,
    last_send, last_recv,
):
    x, strip, y, z, core = place()
    group = x * 2 + core
    count, chans, rows, cols = frames.shape
    channels = [wrap(x + offset, SIDE) for offset in ORDER + (0,)]
    loads = []
    first = pltpu.make_async_copy(depth_hbm, depth, load_sem.at[2 * chans])
    first.start()
    for k, chan in enumerate(channels):
        pair = [
            pltpu.make_async_copy(hbm.at[:, chan], vmem.at[:, chan], load_sem.at[2 * k + j])
            for j, (hbm, vmem) in enumerate(((frames_hbm, frames), (prev_hbm, prev)))
        ]
        for copy in pair:
            copy.start()
        loads.append(pair)

    def of_group(k):
        return (lax.div(k, 2), strip - core + lax.rem(k, 2))

    def of_y(k):
        return (x, (k * 4 + z) * 2 + core)

    def of_z(k):
        return (x, (y * 4 + k) * 2 + core)

    partners = [of_group(wrap(group + k, 8)) for k in range(1, 8)]
    partners += [of_y(wrap(y + k, 4)) for k in range(1, 4)]
    partners += [of_z(wrap(z + k, 4)) for k in range(1, 4)]
    strips = lax.axis_size("pix")
    partners += [(x, wrap(strip + k, strips)) for k in (-1, 1)]
    barrier = pltpu.get_barrier_semaphore()
    for partner in partners:
        pl.semaphore_signal(barrier, inc=1, device_id=partner, device_id_type=MESH)

    def residual(chan, write):
        for f in range(0, count, 8):
            ok = jnp.where(chan == chans - 1, depth[f : f + 8].astype(F32), 1.0)
            value = (
                frames[f : f + 8, chan].astype(F32) - prev[f : f + 8, chan].astype(F32)
            ) * ok
            lay(lines, f, value)
        turned(lines, write, rows)

    args = (x, strip, flat, swapped, swap_send, swap_recv)
    pixels = rows * cols
    halves = (pl.ds(0, pixels // 2), pl.ds(pixels // 2, pixels // 2))
    sends = []
    first.wait()
    for k, offset in enumerate(ORDER):
        for copy in loads[k]:
            copy.wait()

        def write(where, value, chan=channels[k]):
            flat[chan, :, where] = value.astype(BF16)

        residual(channels[k], write)
        if k == 0:
            pl.semaphore_wait(barrier, len(partners))
        sends.append(send_along_x(*args, offset, 0, halves[0]))
        sends[-1].start()
    for offset in ORDER:
        sends.append(send_along_x(*args, offset, 1, halves[1]))
        sends[-1].start()
    for copy in loads[-1]:
        copy.wait()

    def write_own(where, value):
        swapped[x, :, where] = value.astype(BF16)

    residual(x, write_own)

    def write_valid(where, value):
        flat_valid[:, where] = value.astype(BF16)

    lay(lines, 0, depth[...].astype(F32))
    turned(lines, write_valid, rows)
    for chan in range(chans):

        def write_frames(where, value):
            flat_frames[chan, :, where] = value.astype(BF16)

        for f in range(0, count, 8):
            lay(lines, f, frames[f : f + 8, chan].astype(F32))
        turned(lines, write_frames, rows)
    every = count * SIDE
    chunk = 1024
    partial = jnp.zeros((every, every), F32)
    for half in range(2):
        for offset in ORDER:
            taken_along_x(*args, offset, half, halves[half]).wait_recv()
        for start in range(half * pixels // 2, (half + 1) * pixels // 2, chunk):
            block = swapped[:, :, start : start + chunk].reshape(every, chunk)
            partial = partial + lax.dot_general(
                block, block, (((1,), (1,)), ((), ())), preferred_element_type=F32
            )
    for copy in sends:
        copy.wait_send()
    part[...] = partial.reshape(part.shape)

    def exchange(index, size, where, source_of, buffer, send_sem, recv_sem):
        copies = []
        for k in range(1, size):
            to = wrap(index + k, size)
            copies.append(
                pltpu.make_async_remote_copy(
                    src_ref=source_of(to),
                    dst_ref=buffer.at[index],
                    send_sem=send_sem.at[k],
                    recv_sem=recv_sem.at[k],
                    device_id=where(to),
                    device_id_type=MESH,
                )
            )
        for copy in copies:
            copy.start()
        return copies

    def arrive(index, size, where, source_of, buffer, send_sem, recv_sem, copies):
        for k in range(1, size):
            pltpu.make_async_remote_copy(
                src_ref=source_of(wrap(index + k, size)),
                dst_ref=buffer.at[wrap(index - k, size)],
                send_sem=send_sem.at[k],
                recv_sem=recv_sem.at[k],
                device_id=where(wrap(index + k, size)),
                device_id_type=MESH,
            ).wait_recv()
        for copy in copies:
            copy.wait_send()

    def added(buffer, size):
        out = buffer[0]
        for k in range(1, size):
            out = out + buffer[k]
        return out

    args = (group, 8, of_group, lambda k: part.at[k], pieces, first_send, first_recv)
    copies = exchange(*args)
    pieces[group] = part[group]
    arrive(*args, copies)
    in_y[y] = added(pieces, 8)

    args = (y, 4, of_y, lambda k: in_y.at[y], in_y, y_send, y_recv)
    arrive(*args, exchange(*args))
    in_z[z] = added(in_y, 4)

    args = (z, 4, of_z, lambda k: in_z.at[z], in_z, z_send, z_recv)
    arrive(*args, exchange(*args))
    total[group] = added(in_z, 4)

    args = (group, 8, of_group, lambda k: total.at[group], total, last_send, last_recv)
    arrive(*args, exchange(*args))
    return total[...].reshape(every, every)


def exact(left, right, dims):
    return lax.dot_general(
        left, right, (dims, ((), ())), precision=lax.Precision.HIGHEST, preferred_element_type=F32
    )


def lower_solve(square, sides):
    size = square.shape[0]
    blocks = size // 8
    sub = lax.broadcasted_iota(jnp.int32, (8, 128), 0)
    tiles = [square[8 * i : 8 * i + 8, :] for i in range(blocks)]
    hands = [[side[8 * i : 8 * i + 8, :] for i in range(blocks)] for side in sides]
    solved = [[] for _ in sides]
    for b in range(blocks):
        cols = [
            [
                jnp.broadcast_to(tiles[i][:, 8 * b + t : 8 * b + t + 1], (8, 128))
                if i >= b
                else None
                for i in range(blocks)
            ]
            for t in range(8)
        ]
        pivot = [
            [
                jnp.broadcast_to(cols[t][b][u : u + 1, :], (8, 128)) if u >= t else None
                for u in range(8)
            ]
            for t in range(8)
        ]
        rate = []
        low = [[None] * 8 for _ in range(8)]
        for t in range(8):
            rate.append(lax.rsqrt(pivot[t][t]))
            for u in range(t + 1, 8):
                low[u][t] = pivot[t][u] * rate[t]
            for u in range(t + 1, 8):
                for v in range(u, 8):
                    pivot[u][v] = pivot[u][v] - low[u][t] * low[v][t]

        def reduced(rows):
            done = []
            for t in range(8):
                value = rows[t]
                for s in range(t):
                    value = value - done[s] * low[t][s][:, : value.shape[1]]
                done.append(value * rate[t][:, : value.shape[1]])
            return done

        below = {i: reduced([cols[t][i] for t in range(8)]) for i in range(b + 1, blocks)}
        if b + 1 < blocks:
            across = reduced(
                [jnp.broadcast_to(tiles[b][t : t + 1, :], (8, size)) for t in range(8)]
            )
            for i in range(b + 1, blocks):
                for t in range(8):
                    tiles[i] = tiles[i] - below[i][t][:, :size] * across[t]
        for hand, out in zip(hands, solved):
            rows = reduced([jnp.broadcast_to(hand[b][t : t + 1, :], (8, 128)) for t in range(8)])
            tile = rows[0]
            for t in range(1, 8):
                tile = jnp.where(sub == t, rows[t], tile)
            out.append(tile)
            for i in range(b + 1, blocks):
                for t in range(8):
                    hand[i] = hand[i] - below[i][t] * rows[t]
    return [jnp.concatenate(out, axis=0) for out in solved]


def mixing_stage(gram, sketch, gram_sc, basis_sc):
    gram_sc[...] = gram
    basis_sc[...] = sketch

    def turn(step, carry):
        basis = basis_sc[...]
        image = exact(basis, gram_sc[...], ((1,), (1,)))
        square = exact(basis, image, ((1,), (1,)))
        basis_sc[...] = lower_solve(square, [image])[0]
        return carry

    lax.fori_loop(0, POWER, turn, 0)
    basis = basis_sc[...]
    image = exact(basis, gram_sc[...], ((1,), (0,)))
    square = exact(basis, image, ((1,), (1,)))
    left, right = lower_solve(square, [basis, image])
    return exact(right, left, ((0,), (0,))).astype(BF16)


def smooth_channel(
    strips, strip, chan, offset, lam_ref, frames, back, valid, above, below,
    back_out, fore_out, lines_out, source, first, second, between,
):
    lam = lam_ref[chan]
    step = STEP_SIZE / lam
    last = frames.shape[0] - 1
    halo = NSWEEP
    span, lines, cols = source.shape
    rows = span - 2 * halo
    tiles = cols // 128
    lane = lax.broadcasted_iota(jnp.int32, (lines, 128), 1)
    open_above = jnp.where(strip > 0, F32(1.0), F32(0.0))
    open_below = jnp.where(strip < strips - 1, F32(1.0), F32(0.0))

    def tile(ref, r):
        return [ref[r, :, 128 * j : 128 * j + 128] for j in range(tiles)]

    def put(ref, r, values):
        for j in range(tiles):
            ref[r, :, 128 * j : 128 * j + 128] = values[j]

    def unturn(r, values):
        for j in range(tiles):
            lines_out.at[j][pl.ds(r, lines, stride=rows), :] = values[j]

    def unlay(target):
        for j in range(tiles):
            value = lines_out[j].reshape(lines, rows, 128).astype(BF16)
            target[:, chan, :, 128 * j : 128 * j + 128] = value

    for r in range(halo):
        source[r] = above[offset, :, r * cols : (r + 1) * cols].astype(F32) * step
        source[halo + rows + r] = below[offset, :, r * cols : (r + 1) * cols].astype(F32) * step
    for r in range(rows):
        where = slice(r * cols, (r + 1) * cols)
        ok = jnp.where(chan == last, valid[:, where].astype(F32), 1.0)
        held = back[chan, :, where].astype(F32)
        unturn(r, [held[:, 128 * j : 128 * j + 128] for j in range(tiles)])
        source[halo + r] = (frames[chan, :, where].astype(F32) - held) * (ok * step)
    unlay(back_out)

    def before(values):
        turned = [pltpu.roll(v, 1, 1) for v in values]
        return [jnp.where(lane == 0, turned[j - 1] if j else 0.0, turned[j]) for j in range(tiles)]

    def after(values):
        turned = [pltpu.roll(v, 127, 1) for v in values]
        return [jnp.where(lane == 127, turned[j + 1] if j + 1 < tiles else values[j], turned[j]) for j in range(tiles)]

    def image(r, up, here, beside):
        left = before(beside)
        return [s - STEP_SIZE * ((h - u) + (b - l)) for s, u, h, b, l in zip(tile(source, r), up, here, beside, left)]

    def update(r, smooth, under, here, beside):
        right = after(smooth)
        news = []
        for j in range(tiles):
            down = under[j] - smooth[j]
            if r == halo - 1:
                down = down * open_above
            if r == halo + rows - 1:
                down = down * open_below
            across = right[j] - smooth[j]
            square = jnp.maximum(down * down + across * across, 1e-37)
            rate = 1.0 / (1.0 + square * lax.rsqrt(square))
            a = -down if here is None else here[j] - down
            b = -across if beside is None else beside[j] - across
            news.append((a * rate, b * rate))
        put(first, r, [n[0] for n in news])
        put(second, r, [n[1] for n in news])

    smooth = tile(source, 0)
    for r in range(span - 1):
        under = tile(source, r + 1)
        update(r, smooth, under, None, None)
        smooth = under
    for sweep in range(1, NSWEEP):
        between(sweep)
        here, beside = tile(first, sweep), tile(second, sweep)
        smooth = image(sweep, tile(first, sweep - 1), here, beside)
        for r in range(sweep, span - 1 - sweep):
            next_here, next_beside = tile(first, r + 1), tile(second, r + 1)
            under = image(r + 1, here, next_here, next_beside)
            update(r, smooth, under, here, beside)
            smooth, here, beside = under, next_here, next_beside
    for r in range(rows):
        i = halo + r
        values = image(i, tile(first, i - 1), tile(first, i), tile(second, i))
        unturn(r, [v * (lam * (1.0 / STEP_SIZE)) for v in values])
    unlay(fore_out)


def finish_stage(
    lam_ref, swapped, mix, frames, valid, back_out, fore_out, lines_out,
    back, made, top, bottom, above, below, source, first, second,
    local_sem, swap_send, swap_recv, halo_send, halo_recv,
):
    x, strip, _, _, _ = place()
    strips = lax.axis_size("pix")
    up, down = wrap(strip - 1, strips), wrap(strip + 1, strips)
    side, count, pixels = swapped.shape
    width = top.shape[-1]
    cols = source.shape[-1]
    parts = ((0, width), (pixels - width, width), (width, pixels - 2 * width))

    def multiply(part):
        start, size = parts[part]
        for at in range(start, start + size, 512):
            where = slice(at, at + 512)
            block = swapped[:, :, where].reshape(side * count, 512)
            out = jnp.dot(mix, block, preferred_element_type=F32)
            made[:, :, where] = out.astype(BF16).reshape(side, count, 512)

    def send(offset, part):
        to = wrap(x + offset, SIDE)
        where = pl.ds(*parts[part])
        return pltpu.make_async_remote_copy(
            src_ref=made.at[to, :, where],
            dst_ref=back.at[x, :, where],
            send_sem=swap_send.at[offset, part],
            recv_sem=swap_recv.at[offset, part],
            device_id=(to, strip),
            device_id_type=MESH,
        )

    def taken(offset, part):
        origin = wrap(x - offset, SIDE)
        where = pl.ds(*parts[part])
        return pltpu.make_async_remote_copy(
            src_ref=made.at[origin, :, where],
            dst_ref=back.at[origin, :, where],
            send_sem=swap_send.at[offset, part],
            recv_sem=swap_recv.at[offset, part],
            device_id=(origin, strip),
            device_id_type=MESH,
        )

    def halo(offset, way):
        outgoing, incoming, to = ((top, below, up), (bottom, above, down))[way]
        return pltpu.make_async_remote_copy(
            src_ref=outgoing.at[offset],
            dst_ref=incoming.at[offset],
            send_sem=halo_send.at[offset, way],
            recv_sem=halo_recv.at[offset, way],
            device_id=(x, to),
            device_id_type=MESH,
        )

    def forward(offset):
        chan = wrap(x - offset, SIDE)
        if offset:
            taken(offset, 0).wait_recv()
            taken(offset, 1).wait_recv()
        for way, target in ((0, top), (1, bottom)):
            where = slice(parts[way][0], parts[way][0] + width)
            held = back if offset else made
            edge = frames[chan, :, where].astype(F32) - held[chan, :, where].astype(F32)
            ok = jnp.where(chan == side - 1, valid[:, where].astype(F32), 1.0)
            target[offset] = (edge * ok).astype(BF16)
        for way in range(2):
            halo(offset, way).start()

    multiply(0)
    multiply(1)
    forward(0)
    for offset in (1, 3):
        for part in range(2):
            send(offset, part).start()
    multiply(2)
    for offset in (1, 3):
        send(offset, 2).start()
    for part in (0, 1, 2):
        send(2, part).start()
    mine = pltpu.make_async_copy(made.at[x], back.at[x], local_sem)
    mine.start()
    mine.wait()

    def group(k, carry):
        offset = k + jnp.where(k == 2, 1, 0) - jnp.where(k == 3, 1, 0)

        @pl.when(k > 0)
        def _():
            taken(offset, 2).wait_recv()

        for way in range(2):
            halo(offset, way).wait_recv()

        def between(sweep):
            for turn, at, offsets in ((0, 3, (1, 3)), (2, 1, (2,))):
                if sweep == at:

                    @pl.when(k == turn)
                    def _():
                        for offset in offsets:
                            forward(offset)

        smooth_channel(
            strips, strip, wrap(x - offset, SIDE), offset, lam_ref,
            frames, back, valid, above, below, back_out, fore_out, lines_out,
            source, first, second, between,
        )
        return carry

    lax.fori_loop(0, SIDE, group, 0)
    for offset in ORDER:
        for part in range(3):
            send(offset, part).wait_send()
    for offset in range(SIDE):
        for way in range(2):
            halo(offset, way).wait_send()


def whole_kernel(nval, lam_ref, frames_hbm, prev_hbm, depth_hbm, sketch, back, fore, *scratch):
    swapped, flat_frames, flat_valid = scratch[:3]
    gram = gram_stage(frames_hbm, prev_hbm, depth_hbm, *scratch[:24])
    mix = mixing_stage(gram * (1.0 / nval), sketch[...], *scratch[24:26])
    finish_stage(
        lam_ref, swapped, mix, flat_frames, flat_valid, back, fore, scratch[7], *scratch[26:]
    )


def low_rank_and_rest(frames, prev_fg, depth_valid, sketch, lam, nval):
    count, chans, rows, cols = frames.shape
    pixels = rows * cols
    every = count * SIDE
    piece = every // 8
    rank = sketch.shape[1]
    dma = pltpu.SemaphoreType.DMA
    flat = (chans, count, pixels)
    edge = (chans, count, NSWEEP * cols)
    field = (rows + 2 * NSWEEP, count, cols)
    gram_scratch = [
        VMEM(flat, BF16),
        VMEM(flat, BF16),
        VMEM((count, pixels), BF16),
        VMEM(frames.shape, BF16),
        VMEM(frames.shape, BF16),
        VMEM(depth_valid.shape, jnp.int32),
        VMEM(flat, BF16),
        VMEM((cols // 128, count * rows, 128), F32),
        VMEM((8, piece, every), F32),
        VMEM((8, piece, every), F32),
        VMEM((4, piece, every), F32),
        VMEM((4, piece, every), F32),
        VMEM((8, piece, every), F32),
        dma((2 * chans + 1,)),
        dma((4, 2)), dma((4, 2)),
        dma((8,)), dma((8,)),
        dma((4,)), dma((4,)),
        dma((4,)), dma((4,)),
        dma((8,)), dma((8,)),
    ]
    mixing_scratch = [VMEM((every, every), F32), VMEM((rank, every), F32)]
    finish_scratch = [
        VMEM(flat, BF16),
        VMEM(flat, BF16),
        VMEM(edge, BF16),
        VMEM(edge, BF16),
        VMEM(edge, BF16),
        VMEM(edge, BF16),
        VMEM(field, F32),
        VMEM(field, F32),
        VMEM(field, F32),
        dma,
        dma((4, 3)), dma((4, 3)),
        dma((4, 2)), dma((4, 2)),
    ]
    return pl.pallas_call(
        functools.partial(whole_kernel, nval),
        out_shape=(jax.ShapeDtypeStruct(frames.shape, BF16),) * 2,
        in_specs=[pl.BlockSpec(memory_space=pltpu.SMEM)]
        + [pl.BlockSpec(memory_space=pltpu.HBM)] * 3
        + in_vmem(1),
        out_specs=tuple(in_vmem(2)),
        scratch_shapes=gram_scratch + mixing_scratch + finish_scratch,
        compiler_params=pltpu.CompilerParams(
            collective_id=0, has_side_effects=True, vmem_limit_bytes=48 << 20
        ),
        name="godec",
    )(lam, frames, prev_fg, depth_valid, sketch.T)


def local(frames, prev_fg, depth_valid, sketch, tv_weight):
    count, chans, rows, cols = frames.shape
    strips = lax.axis_size("pix")
    nval = chans * rows * strips * cols
    return low_rank_and_rest(frames, prev_fg, depth_valid, sketch, tv_weight, nval)


def solution(mesh):
    placed = (
        P("frame", None, "pix", None),
        P("frame", None, "pix", None),
        P("frame", "pix", None),
        P(),
        P(),
    )
    return jax.shard_map(
        local,
        mesh=mesh,
        in_specs=placed,
        out_specs=(P("frame", None, "pix", None), P("frame", None, "pix", None)),
        check_vma=False,
    )
```

```python
import functools

import jax
import jax.numpy as jnp
from jax import lax
from jax.experimental import pallas as pl
from jax.experimental.pallas import tpu as pltpu
from jax.sharding import PartitionSpec as P

POWER = 3
NSWEEP = 5
STEP_SIZE = 0.125
MESH = pl.DeviceIdType.MESH
VMEM = pltpu.VMEM
SIDE = 4
BF16 = jnp.bfloat16
F32 = jnp.float32


def in_vmem(count):
    return [pl.BlockSpec(memory_space=pltpu.VMEM)] * count


def wrap(value, size):
    return lax.rem(value + size, size)


def place():
    x = lax.axis_index("frame")
    strip = lax.axis_index("pix")
    return x, strip, lax.div(strip, 8), lax.rem(lax.div(strip, 2), 4), lax.rem(strip, 2)


def send_along_x(x, strip, src, dst, send_sem, recv_sem, offset, part, where):
    to = wrap(x + offset, SIDE)
    return pltpu.make_async_remote_copy(
        src_ref=src.at[to, :, where],
        dst_ref=dst.at[x, :, where],
        send_sem=send_sem.at[offset, part],
        recv_sem=recv_sem.at[offset, part],
        device_id=(to, strip),
        device_id_type=MESH,
    )


def taken_along_x(x, strip, src, dst, send_sem, recv_sem, offset, part, where):
    origin = wrap(x - offset, SIDE)
    return pltpu.make_async_remote_copy(
        src_ref=src.at[origin, :, where],
        dst_ref=dst.at[origin, :, where],
        send_sem=send_sem.at[offset, part],
        recv_sem=recv_sem.at[offset, part],
        device_id=(origin, strip),
        device_id_type=MESH,
    )


ORDER = (2, 1, 3)


def lay(lines, start, value):
    count, rows, cols = value.shape
    value = value.reshape(count * rows, cols)
    for j in range(lines.shape[0]):
        lines[j, start * rows : (start + count) * rows, :] = value[:, 128 * j : 128 * j + 128]


def turned(lines, write, rows):
    tiles, size, _ = lines.shape
    for r in range(rows):
        for j in range(tiles):
            start = (r * tiles + j) * 128
            value = lines.at[j][pl.ds(r, size // rows, stride=rows), :]
            write(slice(start, start + 128), value)


def gram_stage(
    frames_hbm, prev_hbm, depth_hbm, swapped, flat_frames, flat_valid, frames, prev, depth, flat, lines, part, pieces, in_y, in_z, total,
    load_sem, swap_send, swap_recv, first_send, first_recv, y_send, y_recv, z_send, z_recv,
    last_send, last_recv,
):
    x, strip, y, z, core = place()
    group = x * 2 + core
    count, chans, rows, cols = frames.shape
    channels = [wrap(x + offset, SIDE) for offset in ORDER + (0,)]
    loads = []
    first = pltpu.make_async_copy(depth_hbm, depth, load_sem.at[2 * chans])
    first.start()
    for k, chan in enumerate(channels):
        pair = [
            pltpu.make_async_copy(hbm.at[:, chan], vmem.at[:, chan], load_sem.at[2 * k + j])
            for j, (hbm, vmem) in enumerate(((frames_hbm, frames), (prev_hbm, prev)))
        ]
        for copy in pair:
            copy.start()
        loads.append(pair)

    def of_group(k):
        return (lax.div(k, 2), strip - core + lax.rem(k, 2))

    def of_y(k):
        return (x, (k * 4 + z) * 2 + core)

    def of_z(k):
        return (x, (y * 4 + k) * 2 + core)

    partners = [of_group(wrap(group + k, 8)) for k in range(1, 8)]
    partners += [of_y(wrap(y + k, 4)) for k in range(1, 4)]
    partners += [of_z(wrap(z + k, 4)) for k in range(1, 4)]
    strips = lax.axis_size("pix")
    partners += [(x, wrap(strip + k, strips)) for k in (-1, 1)]
    barrier = pltpu.get_barrier_semaphore()
    for partner in partners:
        pl.semaphore_signal(barrier, inc=1, device_id=partner, device_id_type=MESH)

    def residual(chan, write):
        for f in range(0, count, 8):
            ok = jnp.where(chan == chans - 1, depth[f : f + 8].astype(F32), 1.0)
            value = (
                frames[f : f + 8, chan].astype(F32) - prev[f : f + 8, chan].astype(F32)
            ) * ok
            lay(lines, f, value)
        turned(lines, write, rows)

    args = (x, strip, flat, swapped, swap_send, swap_recv)
    pixels = rows * cols
    halves = (pl.ds(0, pixels // 2), pl.ds(pixels // 2, pixels // 2))
    sends = []
    first.wait()
    for k, offset in enumerate(ORDER):
        for copy in loads[k]:
            copy.wait()

        def write(where, value, chan=channels[k]):
            flat[chan, :, where] = value.astype(BF16)

        residual(channels[k], write)
        if k == 0:
            pl.semaphore_wait(barrier, len(partners))
        sends.append(send_along_x(*args, offset, 0, halves[0]))
        sends[-1].start()
    for offset in ORDER:
        sends.append(send_along_x(*args, offset, 1, halves[1]))
        sends[-1].start()
    for copy in loads[-1]:
        copy.wait()

    def write_own(where, value):
        swapped[x, :, where] = value.astype(BF16)

    residual(x, write_own)

    def write_valid(where, value):
        flat_valid[:, where] = value.astype(BF16)

    lay(lines, 0, depth[...].astype(F32))
    turned(lines, write_valid, rows)
    for chan in range(chans):

        def write_frames(where, value):
            flat_frames[chan, :, where] = value.astype(BF16)

        for f in range(0, count, 8):
            lay(lines, f, frames[f : f + 8, chan].astype(F32))
        turned(lines, write_frames, rows)
    every = count * SIDE
    chunk = 1024
    partial = jnp.zeros((every, every), F32)
    for half in range(2):
        for offset in ORDER:
            taken_along_x(*args, offset, half, halves[half]).wait_recv()
        for start in range(half * pixels // 2, (half + 1) * pixels // 2, chunk):
            block = swapped[:, :, start : start + chunk].reshape(every, chunk)
            partial = partial + lax.dot_general(
                block, block, (((1,), (1,)), ((), ())), preferred_element_type=F32
            )
    for copy in sends:
        copy.wait_send()
    part[...] = partial.reshape(part.shape)

    def exchange(index, size, where, source_of, buffer, send_sem, recv_sem):
        copies = []
        for k in range(1, size):
            to = wrap(index + k, size)
            copies.append(
                pltpu.make_async_remote_copy(
                    src_ref=source_of(to),
                    dst_ref=buffer.at[index],
                    send_sem=send_sem.at[k],
                    recv_sem=recv_sem.at[k],
                    device_id=where(to),
                    device_id_type=MESH,
                )
            )
        for copy in copies:
            copy.start()
        return copies

    def arrive(index, size, where, source_of, buffer, send_sem, recv_sem, copies):
        for k in range(1, size):
            pltpu.make_async_remote_copy(
                src_ref=source_of(wrap(index + k, size)),
                dst_ref=buffer.at[wrap(index - k, size)],
                send_sem=send_sem.at[k],
                recv_sem=recv_sem.at[k],
                device_id=where(wrap(index + k, size)),
                device_id_type=MESH,
            ).wait_recv()
        for copy in copies:
            copy.wait_send()

    def added(buffer, size):
        out = buffer[0]
        for k in range(1, size):
            out = out + buffer[k]
        return out

    args = (group, 8, of_group, lambda k: part.at[k], pieces, first_send, first_recv)
    copies = exchange(*args)
    pieces[group] = part[group]
    arrive(*args, copies)
    in_y[y] = added(pieces, 8)

    args = (y, 4, of_y, lambda k: in_y.at[y], in_y, y_send, y_recv)
    arrive(*args, exchange(*args))
    in_z[z] = added(in_y, 4)

    args = (z, 4, of_z, lambda k: in_z.at[z], in_z, z_send, z_recv)
    arrive(*args, exchange(*args))
    total[group] = added(in_z, 4)

    args = (group, 8, of_group, lambda k: total.at[group], total, last_send, last_recv)
    arrive(*args, exchange(*args))
    return total[...].reshape(every, every)


def exact(left, right, dims):
    return lax.dot_general(
        left, right, (dims, ((), ())), precision=lax.Precision.HIGHEST, preferred_element_type=F32
    )


def lower_solve(square, sides):
    size = square.shape[0]
    blocks = size // 8
    sub = lax.broadcasted_iota(jnp.int32, (8, 128), 0)
    tiles = [square[8 * i : 8 * i + 8, :] for i in range(blocks)]
    hands = [[side[8 * i : 8 * i + 8, :] for i in range(blocks)] for side in sides]
    solved = [[] for _ in sides]
    for b in range(blocks):
        cols = [
            [
                jnp.broadcast_to(tiles[i][:, 8 * b + t : 8 * b + t + 1], (8, 128))
                if i >= b
                else None
                for i in range(blocks)
            ]
            for t in range(8)
        ]
        pivot = [
            [
                jnp.broadcast_to(cols[t][b][u : u + 1, :], (8, 128)) if u >= t else None
                for u in range(8)
            ]
            for t in range(8)
        ]
        rate = []
        low = [[None] * 8 for _ in range(8)]
        for t in range(8):
            rate.append(lax.rsqrt(pivot[t][t]))
            for u in range(t + 1, 8):
                low[u][t] = pivot[t][u] * rate[t]
            for u in range(t + 1, 8):
                for v in range(u, 8):
                    pivot[u][v] = pivot[u][v] - low[u][t] * low[v][t]

        def reduced(rows):
            done = []
            for t in range(8):
                value = rows[t]
                for s in range(t):
                    value = value - done[s] * low[t][s][:, : value.shape[1]]
                done.append(value * rate[t][:, : value.shape[1]])
            return done

        below = {i: reduced([cols[t][i] for t in range(8)]) for i in range(b + 1, blocks)}
        if b + 1 < blocks:
            across = reduced(
                [jnp.broadcast_to(tiles[b][t : t + 1, :], (8, size)) for t in range(8)]
            )
            for i in range(b + 1, blocks):
                for t in range(8):
                    tiles[i] = tiles[i] - below[i][t][:, :size] * across[t]
        for hand, out in zip(hands, solved):
            rows = reduced([jnp.broadcast_to(hand[b][t : t + 1, :], (8, 128)) for t in range(8)])
            tile = rows[0]
            for t in range(1, 8):
                tile = jnp.where(sub == t, rows[t], tile)
            out.append(tile)
            for i in range(b + 1, blocks):
                for t in range(8):
                    hand[i] = hand[i] - below[i][t] * rows[t]
    return [jnp.concatenate(out, axis=0) for out in solved]


def mixing_stage(gram, gram_sc, basis_sc):
    gram_sc[...] = gram

    def turn(step, carry):
        basis = basis_sc[...]
        image = exact(basis, gram_sc[...], ((1,), (1,)))
        square = exact(basis, image, ((1,), (1,)))
        basis_sc[...] = lower_solve(square, [image])[0]
        return carry

    lax.fori_loop(0, POWER, turn, 0)
    basis = basis_sc[...]
    image = exact(basis, gram_sc[...], ((1,), (0,)))
    square = exact(basis, image, ((1,), (1,)))
    left, right = lower_solve(square, [basis, image])
    return exact(right, left, ((0,), (0,))).astype(BF16)


def smooth_channel(
    strips, strip, chan, offset, lam_ref, frames, back, valid, above, below,
    back_out, fore_out, lines_out, source, first, second, between,
):
    lam = lam_ref[chan]
    step = STEP_SIZE / lam
    last = frames.shape[0] - 1
    halo = NSWEEP
    span, lines, cols = source.shape
    rows = span - 2 * halo
    tiles = cols // 128
    lane = lax.broadcasted_iota(jnp.int32, (lines, 128), 1)
    open_above = jnp.where(strip > 0, F32(1.0), F32(0.0))
    open_below = jnp.where(strip < strips - 1, F32(1.0), F32(0.0))

    def tile(ref, r):
        return [ref[r, :, 128 * j : 128 * j + 128] for j in range(tiles)]

    def put(ref, r, values):
        for j in range(tiles):
            ref[r, :, 128 * j : 128 * j + 128] = values[j]

    def unturn(r, values):
        for j in range(tiles):
            lines_out.at[j][pl.ds(r, lines, stride=rows), :] = values[j]

    def unlay(target):
        for j in range(tiles):
            value = lines_out[j].reshape(lines, rows, 128).astype(BF16)
            target[:, chan, :, 128 * j : 128 * j + 128] = value

    for r in range(halo):
        source[r] = above[offset, :, r * cols : (r + 1) * cols].astype(F32) * step
        source[halo + rows + r] = below[offset, :, r * cols : (r + 1) * cols].astype(F32) * step
    for r in range(rows):
        where = slice(r * cols, (r + 1) * cols)
        ok = jnp.where(chan == last, valid[:, where].astype(F32), 1.0)
        held = back[chan, :, where].astype(F32)
        unturn(r, [held[:, 128 * j : 128 * j + 128] for j in range(tiles)])
        source[halo + r] = (frames[chan, :, where].astype(F32) - held) * (ok * step)
    unlay(back_out)

    def before(values):
        turned = [pltpu.roll(v, 1, 1) for v in values]
        return [jnp.where(lane == 0, turned[j - 1] if j else 0.0, turned[j]) for j in range(tiles)]

    def after(values):
        turned = [pltpu.roll(v, 127, 1) for v in values]
        return [jnp.where(lane == 127, turned[j + 1] if j + 1 < tiles else values[j], turned[j]) for j in range(tiles)]

    def image(r, up, here, beside):
        left = before(beside)
        return [s - STEP_SIZE * ((h - u) + (b - l)) for s, u, h, b, l in zip(tile(source, r), up, here, beside, left)]

    def update(r, smooth, under, here, beside):
        right = after(smooth)
        news = []
        for j in range(tiles):
            down = under[j] - smooth[j]
            if r == halo - 1:
                down = down * open_above
            if r == halo + rows - 1:
                down = down * open_below
            across = right[j] - smooth[j]
            square = jnp.maximum(down * down + across * across, 1e-37)
            rate = 1.0 / (1.0 + square * lax.rsqrt(square))
            a = -down if here is None else here[j] - down
            b = -across if beside is None else beside[j] - across
            news.append((a * rate, b * rate))
        put(first, r, [n[0] for n in news])
        put(second, r, [n[1] for n in news])

    smooth = tile(source, 0)
    for r in range(span - 1):
        under = tile(source, r + 1)
        update(r, smooth, under, None, None)
        smooth = under
    for sweep in range(1, NSWEEP):
        between(sweep)
        here, beside = tile(first, sweep), tile(second, sweep)
        smooth = image(sweep, tile(first, sweep - 1), here, beside)
        for r in range(sweep, span - 1 - sweep):
            next_here, next_beside = tile(first, r + 1), tile(second, r + 1)
            under = image(r + 1, here, next_here, next_beside)
            update(r, smooth, under, here, beside)
            smooth, here, beside = under, next_here, next_beside
    for r in range(rows):
        i = halo + r
        values = image(i, tile(first, i - 1), tile(first, i), tile(second, i))
        unturn(r, [v * (lam * (1.0 / STEP_SIZE)) for v in values])
    unlay(fore_out)


def finish_stage(
    lam_ref, swapped, mix, frames, valid, back_out, fore_out, lines_out,
    back, made, top, bottom, above, below, source, first, second,
    local_sem, swap_send, swap_recv, halo_send, halo_recv,
):
    x, strip, _, _, _ = place()
    strips = lax.axis_size("pix")
    up, down = wrap(strip - 1, strips), wrap(strip + 1, strips)
    side, count, pixels = swapped.shape
    width = top.shape[-1]
    cols = source.shape[-1]
    parts = ((0, width), (pixels - width, width), (width, pixels - 2 * width))

    def multiply(part):
        start, size = parts[part]
        for at in range(start, start + size, 512):
            where = slice(at, at + 512)
            block = swapped[:, :, where].reshape(side * count, 512)
            out = jnp.dot(mix, block, preferred_element_type=F32)
            made[:, :, where] = out.astype(BF16).reshape(side, count, 512)

    def send(offset, part):
        to = wrap(x + offset, SIDE)
        where = pl.ds(*parts[part])
        return pltpu.make_async_remote_copy(
            src_ref=made.at[to, :, where],
            dst_ref=back.at[x, :, where],
            send_sem=swap_send.at[offset, part],
            recv_sem=swap_recv.at[offset, part],
            device_id=(to, strip),
            device_id_type=MESH,
        )

    def taken(offset, part):
        origin = wrap(x - offset, SIDE)
        where = pl.ds(*parts[part])
        return pltpu.make_async_remote_copy(
            src_ref=made.at[origin, :, where],
            dst_ref=back.at[origin, :, where],
            send_sem=swap_send.at[offset, part],
            recv_sem=swap_recv.at[offset, part],
            device_id=(origin, strip),
            device_id_type=MESH,
        )

    def halo(offset, way):
        outgoing, incoming, to = ((top, below, up), (bottom, above, down))[way]
        return pltpu.make_async_remote_copy(
            src_ref=outgoing.at[offset],
            dst_ref=incoming.at[offset],
            send_sem=halo_send.at[offset, way],
            recv_sem=halo_recv.at[offset, way],
            device_id=(x, to),
            device_id_type=MESH,
        )

    def forward(offset):
        chan = wrap(x - offset, SIDE)
        if offset:
            taken(offset, 0).wait_recv()
            taken(offset, 1).wait_recv()
        for way, target in ((0, top), (1, bottom)):
            where = slice(parts[way][0], parts[way][0] + width)
            held = back if offset else made
            edge = frames[chan, :, where].astype(F32) - held[chan, :, where].astype(F32)
            ok = jnp.where(chan == side - 1, valid[:, where].astype(F32), 1.0)
            target[offset] = (edge * ok).astype(BF16)
        for way in range(2):
            halo(offset, way).start()

    multiply(0)
    multiply(1)
    forward(0)
    for offset in (1, 3):
        for part in range(2):
            send(offset, part).start()
    multiply(2)
    for offset in (1, 3):
        send(offset, 2).start()
    for part in (0, 1, 2):
        send(2, part).start()
    mine = pltpu.make_async_copy(made.at[x], back.at[x], local_sem)
    mine.start()
    mine.wait()

    def group(k, carry):
        offset = k + jnp.where(k == 2, 1, 0) - jnp.where(k == 3, 1, 0)

        @pl.when(k > 0)
        def _():
            taken(offset, 2).wait_recv()

        for way in range(2):
            halo(offset, way).wait_recv()

        def between(sweep):
            for turn, at, offsets in ((0, 3, (1, 3)), (2, 1, (2,))):
                if sweep == at:

                    @pl.when(k == turn)
                    def _():
                        for offset in offsets:
                            forward(offset)

        smooth_channel(
            strips, strip, wrap(x - offset, SIDE), offset, lam_ref,
            frames, back, valid, above, below, back_out, fore_out, lines_out,
            source, first, second, between,
        )
        return carry

    lax.fori_loop(0, SIDE, group, 0)
    for offset in ORDER:
        for part in range(3):
            send(offset, part).wait_send()
    for offset in range(SIDE):
        for way in range(2):
            halo(offset, way).wait_send()


def whole_kernel(
    nval, lam_hbm, frames_hbm, prev_hbm, depth_hbm, sketch_hbm, back, fore, lam_ref, small_sem,
    *scratch
):
    swapped, flat_frames, flat_valid = scratch[:3]
    basis_sc = scratch[25]
    small = [
        pltpu.make_async_copy(lam_hbm, lam_ref, small_sem.at[0]),
        pltpu.make_async_copy(sketch_hbm, basis_sc, small_sem.at[1]),
    ]
    for copy in small:
        copy.start()
    gram = gram_stage(frames_hbm, prev_hbm, depth_hbm, *scratch[:24])
    for copy in small:
        copy.wait()
    mix = mixing_stage(gram * (1.0 / nval), *scratch[24:26])
    finish_stage(
        lam_ref, swapped, mix, flat_frames, flat_valid, back, fore, scratch[7], *scratch[26:]
    )


def low_rank_and_rest(frames, prev_fg, depth_valid, sketch, lam, nval):
    count, chans, rows, cols = frames.shape
    pixels = rows * cols
    every = count * SIDE
    piece = every // 8
    rank = sketch.shape[1]
    dma = pltpu.SemaphoreType.DMA
    flat = (chans, count, pixels)
    edge = (chans, count, NSWEEP * cols)
    field = (rows + 2 * NSWEEP, count, cols)
    gram_scratch = [
        VMEM(flat, BF16),
        VMEM(flat, BF16),
        VMEM((count, pixels), BF16),
        VMEM(frames.shape, BF16),
        VMEM(frames.shape, BF16),
        VMEM(depth_valid.shape, jnp.int32),
        VMEM(flat, BF16),
        VMEM((cols // 128, count * rows, 128), F32),
        VMEM((8, piece, every), F32),
        VMEM((8, piece, every), F32),
        VMEM((4, piece, every), F32),
        VMEM((4, piece, every), F32),
        VMEM((8, piece, every), F32),
        dma((2 * chans + 1,)),
        dma((4, 2)), dma((4, 2)),
        dma((8,)), dma((8,)),
        dma((4,)), dma((4,)),
        dma((4,)), dma((4,)),
        dma((8,)), dma((8,)),
    ]
    mixing_scratch = [VMEM((every, every), F32), VMEM((rank, every), F32)]
    finish_scratch = [
        VMEM(flat, BF16),
        VMEM(flat, BF16),
        VMEM(edge, BF16),
        VMEM(edge, BF16),
        VMEM(edge, BF16),
        VMEM(edge, BF16),
        VMEM(field, F32),
        VMEM(field, F32),
        VMEM(field, F32),
        dma,
        dma((4, 3)), dma((4, 3)),
        dma((4, 2)), dma((4, 2)),
    ]
    return pl.pallas_call(
        functools.partial(whole_kernel, nval),
        out_shape=(jax.ShapeDtypeStruct(frames.shape, BF16),) * 2,
        in_specs=[pl.BlockSpec(memory_space=pltpu.HBM)] * 5,
        out_specs=tuple(in_vmem(2)),
        scratch_shapes=[pltpu.SMEM((chans,), F32), dma((2,))]
        + gram_scratch
        + mixing_scratch
        + finish_scratch,
        compiler_params=pltpu.CompilerParams(
            collective_id=0, has_side_effects=True, vmem_limit_bytes=48 << 20
        ),
        name="godec",
    )(*[pltpu.with_memory_space_constraint(v, pltpu.HBM) for v in (lam, frames, prev_fg, depth_valid, sketch.T)])


def local(frames, prev_fg, depth_valid, sketch, tv_weight):
    count, chans, rows, cols = frames.shape
    strips = lax.axis_size("pix")
    nval = chans * rows * strips * cols
    return low_rank_and_rest(frames, prev_fg, depth_valid, sketch, tv_weight, nval)


def solution(mesh):
    placed = (
        P("frame", None, "pix", None),
        P("frame", None, "pix", None),
        P("frame", "pix", None),
        P(),
        P(),
    )
    return jax.shard_map(
        local,
        mesh=mesh,
        in_specs=placed,
        out_specs=(P("frame", None, "pix", None), P("frame", None, "pix", None)),
        check_vma=False,
    )
```

```python
import functools

import jax
import jax.numpy as jnp
from jax import lax
from jax.experimental import pallas as pl
from jax.experimental.pallas import tpu as pltpu
from jax.sharding import PartitionSpec as P

POWER = 3
NSWEEP = 5
STEP_SIZE = 0.125
MESH = pl.DeviceIdType.MESH
VMEM = pltpu.VMEM
SIDE = 4
BF16 = jnp.bfloat16
F32 = jnp.float32


def in_vmem(count):
    return [pl.BlockSpec(memory_space=pltpu.VMEM)] * count


def wrap(value, size):
    return lax.rem(value + size, size)


def place():
    x = lax.axis_index("frame")
    strip = lax.axis_index("pix")
    return x, strip, lax.div(strip, 8), lax.rem(lax.div(strip, 2), 4), lax.rem(strip, 2)


def send_along_x(x, strip, src, dst, send_sem, recv_sem, offset, part, where):
    to = wrap(x + offset, SIDE)
    return pltpu.make_async_remote_copy(
        src_ref=src.at[to, :, where],
        dst_ref=dst.at[x, :, where],
        send_sem=send_sem.at[offset, part],
        recv_sem=recv_sem.at[offset, part],
        device_id=(to, strip),
        device_id_type=MESH,
    )


def taken_along_x(x, strip, src, dst, send_sem, recv_sem, offset, part, where):
    origin = wrap(x - offset, SIDE)
    return pltpu.make_async_remote_copy(
        src_ref=src.at[origin, :, where],
        dst_ref=dst.at[origin, :, where],
        send_sem=send_sem.at[offset, part],
        recv_sem=recv_sem.at[offset, part],
        device_id=(origin, strip),
        device_id_type=MESH,
    )


ORDER = (2, 1, 3)


def lay(lines, start, value):
    count, rows, cols = value.shape
    value = value.reshape(count * rows, cols)
    for j in range(lines.shape[0]):
        lines[j, start * rows : (start + count) * rows, :] = value[:, 128 * j : 128 * j + 128]


def turned(lines, write, rows):
    tiles, size, _ = lines.shape
    for r in range(rows):
        for j in range(tiles):
            start = (r * tiles + j) * 128
            value = lines.at[j][pl.ds(r, size // rows, stride=rows), :]
            write(slice(start, start + 128), value)


def gram_stage(
    frames_hbm, prev_hbm, depth_hbm, swapped, flat_frames, flat_valid, frames, prev, depth, flat, lines, part, pieces, in_plane, total,
    load_sem, swap_send, swap_recv, first_send, first_recv, plane_send, plane_recv,
    last_send, last_recv,
):
    x, strip, y, z, core = place()
    group = x * 2 + core
    count, chans, rows, cols = frames.shape
    channels = [wrap(x + offset, SIDE) for offset in ORDER + (0,)]
    loads = []
    first = pltpu.make_async_copy(depth_hbm, depth, load_sem.at[2 * chans])
    first.start()
    for k, chan in enumerate(channels):
        pair = [
            pltpu.make_async_copy(hbm.at[:, chan], vmem.at[:, chan], load_sem.at[2 * k + j])
            for j, (hbm, vmem) in enumerate(((frames_hbm, frames), (prev_hbm, prev)))
        ]
        for copy in pair:
            copy.start()
        loads.append(pair)

    def of_group(k):
        return (lax.div(k, 2), strip - core + lax.rem(k, 2))

    plane = y * 4 + z

    def of_plane(k):
        return (x, k * 2 + core)

    partners = [of_group(wrap(group + k, 8)) for k in range(1, 8)]
    partners += [of_plane(wrap(plane + k, 16)) for k in range(1, 16)]
    strips = lax.axis_size("pix")
    partners += [(x, wrap(strip + k, strips)) for k in (-1, 1)]
    barrier = pltpu.get_barrier_semaphore()
    for partner in partners:
        pl.semaphore_signal(barrier, inc=1, device_id=partner, device_id_type=MESH)

    def residual(chan, write):
        for f in range(0, count, 8):
            ok = jnp.where(chan == chans - 1, depth[f : f + 8].astype(F32), 1.0)
            value = (
                frames[f : f + 8, chan].astype(F32) - prev[f : f + 8, chan].astype(F32)
            ) * ok
            lay(lines, f, value)
        turned(lines, write, rows)

    args = (x, strip, flat, swapped, swap_send, swap_recv)
    pixels = rows * cols
    halves = (pl.ds(0, pixels // 2), pl.ds(pixels // 2, pixels // 2))
    sends = []
    first.wait()
    for k, offset in enumerate(ORDER):
        for copy in loads[k]:
            copy.wait()

        def write(where, value, chan=channels[k]):
            flat[chan, :, where] = value.astype(BF16)

        residual(channels[k], write)
        if k == 0:
            pl.semaphore_wait(barrier, len(partners))
        sends.append(send_along_x(*args, offset, 0, halves[0]))
        sends[-1].start()
    for offset in ORDER:
        sends.append(send_along_x(*args, offset, 1, halves[1]))
        sends[-1].start()
    for copy in loads[-1]:
        copy.wait()

    def write_own(where, value):
        swapped[x, :, where] = value.astype(BF16)

    residual(x, write_own)

    def write_valid(where, value):
        flat_valid[:, where] = value.astype(BF16)

    lay(lines, 0, depth[...].astype(F32))
    turned(lines, write_valid, rows)
    for chan in range(chans):

        def write_frames(where, value):
            flat_frames[chan, :, where] = value.astype(BF16)

        for f in range(0, count, 8):
            lay(lines, f, frames[f : f + 8, chan].astype(F32))
        turned(lines, write_frames, rows)
    every = count * SIDE
    chunk = 1024
    partial = jnp.zeros((every, every), F32)
    for half in range(2):
        for offset in ORDER:
            taken_along_x(*args, offset, half, halves[half]).wait_recv()
        for start in range(half * pixels // 2, (half + 1) * pixels // 2, chunk):
            block = swapped[:, :, start : start + chunk].reshape(every, chunk)
            partial = partial + lax.dot_general(
                block, block, (((1,), (1,)), ((), ())), preferred_element_type=F32
            )
    for copy in sends:
        copy.wait_send()
    part[...] = partial.reshape(part.shape)

    def exchange(index, size, where, source_of, buffer, send_sem, recv_sem):
        copies = []
        for k in range(1, size):
            to = wrap(index + k, size)
            copies.append(
                pltpu.make_async_remote_copy(
                    src_ref=source_of(to),
                    dst_ref=buffer.at[index],
                    send_sem=send_sem.at[k],
                    recv_sem=recv_sem.at[k],
                    device_id=where(to),
                    device_id_type=MESH,
                )
            )
        for copy in copies:
            copy.start()
        return copies

    def arrive(index, size, where, source_of, buffer, send_sem, recv_sem, copies):
        for k in range(1, size):
            pltpu.make_async_remote_copy(
                src_ref=source_of(wrap(index + k, size)),
                dst_ref=buffer.at[wrap(index - k, size)],
                send_sem=send_sem.at[k],
                recv_sem=recv_sem.at[k],
                device_id=where(wrap(index + k, size)),
                device_id_type=MESH,
            ).wait_recv()
        for copy in copies:
            copy.wait_send()

    def added(buffer, size):
        out = buffer[0]
        for k in range(1, size):
            out = out + buffer[k]
        return out

    args = (group, 8, of_group, lambda k: part.at[k], pieces, first_send, first_recv)
    copies = exchange(*args)
    pieces[group] = part[group]
    arrive(*args, copies)
    in_plane[plane] = added(pieces, 8)

    args = (plane, 16, of_plane, lambda k: in_plane.at[plane], in_plane, plane_send, plane_recv)
    arrive(*args, exchange(*args))
    total[group] = added(in_plane, 16)

    args = (group, 8, of_group, lambda k: total.at[group], total, last_send, last_recv)
    arrive(*args, exchange(*args))
    return total[...].reshape(every, every)


def exact(left, right, dims):
    return lax.dot_general(
        left, right, (dims, ((), ())), precision=lax.Precision.HIGHEST, preferred_element_type=F32
    )


def lower_solve(square, sides):
    size = square.shape[0]
    blocks = size // 8
    sub = lax.broadcasted_iota(jnp.int32, (8, 128), 0)
    tiles = [square[8 * i : 8 * i + 8, :] for i in range(blocks)]
    hands = [[side[8 * i : 8 * i + 8, :] for i in range(blocks)] for side in sides]
    solved = [[] for _ in sides]
    for b in range(blocks):
        cols = [
            [
                jnp.broadcast_to(tiles[i][:, 8 * b + t : 8 * b + t + 1], (8, 128))
                if i >= b
                else None
                for i in range(blocks)
            ]
            for t in range(8)
        ]
        pivot = [
            [
                jnp.broadcast_to(cols[t][b][u : u + 1, :], (8, 128)) if u >= t else None
                for u in range(8)
            ]
            for t in range(8)
        ]
        rate = []
        low = [[None] * 8 for _ in range(8)]
        for t in range(8):
            rate.append(lax.rsqrt(pivot[t][t]))
            for u in range(t + 1, 8):
                low[u][t] = pivot[t][u] * rate[t]
            for u in range(t + 1, 8):
                for v in range(u, 8):
                    pivot[u][v] = pivot[u][v] - low[u][t] * low[v][t]

        def reduced(rows):
            done = []
            for t in range(8):
                value = rows[t]
                for s in range(t):
                    value = value - done[s] * low[t][s][:, : value.shape[1]]
                done.append(value * rate[t][:, : value.shape[1]])
            return done

        below = {i: reduced([cols[t][i] for t in range(8)]) for i in range(b + 1, blocks)}
        if b + 1 < blocks:
            across = reduced(
                [jnp.broadcast_to(tiles[b][t : t + 1, :], (8, size)) for t in range(8)]
            )
            for i in range(b + 1, blocks):
                for t in range(8):
                    tiles[i] = tiles[i] - below[i][t][:, :size] * across[t]
        for hand, out in zip(hands, solved):
            rows = reduced([jnp.broadcast_to(hand[b][t : t + 1, :], (8, 128)) for t in range(8)])
            tile = rows[0]
            for t in range(1, 8):
                tile = jnp.where(sub == t, rows[t], tile)
            out.append(tile)
            for i in range(b + 1, blocks):
                for t in range(8):
                    hand[i] = hand[i] - below[i][t] * rows[t]
    return [jnp.concatenate(out, axis=0) for out in solved]


def mixing_stage(gram, gram_sc, basis_sc):
    gram_sc[...] = gram

    def turn(step, carry):
        basis = basis_sc[...]
        image = exact(basis, gram_sc[...], ((1,), (1,)))
        square = exact(basis, image, ((1,), (1,)))
        basis_sc[...] = lower_solve(square, [image])[0]
        return carry

    lax.fori_loop(0, POWER, turn, 0)
    basis = basis_sc[...]
    image = exact(basis, gram_sc[...], ((1,), (0,)))
    square = exact(basis, image, ((1,), (1,)))
    left, right = lower_solve(square, [basis, image])
    return exact(right, left, ((0,), (0,))).astype(BF16)


def smooth_channel(
    strips, strip, chan, offset, lam_ref, frames, back, valid, above, below,
    back_out, fore_out, lines_out, source, first, second, edges_here, between,
):
    lam = lam_ref[chan]
    step = STEP_SIZE / lam
    last = frames.shape[0] - 1
    halo = NSWEEP
    span, lines, cols = source.shape
    rows = span - 2 * halo
    tiles = cols // 128
    lane = lax.broadcasted_iota(jnp.int32, (lines, 128), 1)
    open_above = jnp.where(strip > 0, F32(1.0), F32(0.0))
    open_below = jnp.where(strip < strips - 1, F32(1.0), F32(0.0))

    def tile(ref, r):
        return [ref[r, :, 128 * j : 128 * j + 128] for j in range(tiles)]

    def put(ref, r, values):
        for j in range(tiles):
            ref[r, :, 128 * j : 128 * j + 128] = values[j]

    def unturn(r, values):
        for j in range(tiles):
            lines_out.at[j][pl.ds(r, lines, stride=rows), :] = values[j]

    def unlay(target):
        for j in range(tiles):
            value = lines_out[j].reshape(lines, rows, 128).astype(BF16)
            target[:, chan, :, 128 * j : 128 * j + 128] = value

    for r in range(rows):
        where = slice(r * cols, (r + 1) * cols)
        ok = jnp.where(chan == last, valid[:, where].astype(F32), 1.0)
        held = back[chan, :, where].astype(F32)
        unturn(r, [held[:, 128 * j : 128 * j + 128] for j in range(tiles)])
        source[halo + r] = (frames[chan, :, where].astype(F32) - held) * (ok * step)
    unlay(back_out)
    edges_here()
    for r in range(halo):
        source[r] = above[offset, :, r * cols : (r + 1) * cols].astype(F32) * step
        source[halo + rows + r] = below[offset, :, r * cols : (r + 1) * cols].astype(F32) * step

    def before(values):
        turned = [pltpu.roll(v, 1, 1) for v in values]
        return [jnp.where(lane == 0, turned[j - 1] if j else 0.0, turned[j]) for j in range(tiles)]

    def after(values):
        turned = [pltpu.roll(v, 127, 1) for v in values]
        return [jnp.where(lane == 127, turned[j + 1] if j + 1 < tiles else values[j], turned[j]) for j in range(tiles)]

    def image(r, up, here, beside):
        left = before(beside)
        return [s - STEP_SIZE * ((h - u) + (b - l)) for s, u, h, b, l in zip(tile(source, r), up, here, beside, left)]

    def update(r, smooth, under, here, beside):
        right = after(smooth)
        news = []
        for j in range(tiles):
            down = under[j] - smooth[j]
            if r == halo - 1:
                down = down * open_above
            if r == halo + rows - 1:
                down = down * open_below
            across = right[j] - smooth[j]
            square = jnp.maximum(down * down + across * across, 1e-37)
            rate = 1.0 / (1.0 + square * lax.rsqrt(square))
            a = -down if here is None else here[j] - down
            b = -across if beside is None else beside[j] - across
            news.append((a * rate, b * rate))
        put(first, r, [n[0] for n in news])
        put(second, r, [n[1] for n in news])

    smooth = tile(source, 0)
    for r in range(span - 1):
        under = tile(source, r + 1)
        update(r, smooth, under, None, None)
        smooth = under
    for sweep in range(1, NSWEEP):
        between(sweep)
        here, beside = tile(first, sweep), tile(second, sweep)
        smooth = image(sweep, tile(first, sweep - 1), here, beside)
        for r in range(sweep, span - 1 - sweep):
            next_here, next_beside = tile(first, r + 1), tile(second, r + 1)
            under = image(r + 1, here, next_here, next_beside)
            update(r, smooth, under, here, beside)
            smooth, here, beside = under, next_here, next_beside
    for r in range(rows):
        i = halo + r
        values = image(i, tile(first, i - 1), tile(first, i), tile(second, i))
        unturn(r, [v * (lam * (1.0 / STEP_SIZE)) for v in values])
    unlay(fore_out)


def finish_stage(
    lam_ref, swapped, mix, frames, valid, back_out, fore_out, lines_out,
    back, made, top, bottom, above, below, source, first, second,
    local_sem, swap_send, swap_recv, halo_send, halo_recv,
):
    x, strip, _, _, _ = place()
    strips = lax.axis_size("pix")
    up, down = wrap(strip - 1, strips), wrap(strip + 1, strips)
    side, count, pixels = swapped.shape
    width = top.shape[-1]
    cols = source.shape[-1]
    parts = ((0, width), (pixels - width, width), (width, pixels - 2 * width))

    def multiply(part):
        start, size = parts[part]
        for at in range(start, start + size, 512):
            where = slice(at, at + 512)
            block = swapped[:, :, where].reshape(side * count, 512)
            out = jnp.dot(mix, block, preferred_element_type=F32)
            made[:, :, where] = out.astype(BF16).reshape(side, count, 512)

    def send(offset, part):
        to = wrap(x + offset, SIDE)
        where = pl.ds(*parts[part])
        return pltpu.make_async_remote_copy(
            src_ref=made.at[to, :, where],
            dst_ref=back.at[x, :, where],
            send_sem=swap_send.at[offset, part],
            recv_sem=swap_recv.at[offset, part],
            device_id=(to, strip),
            device_id_type=MESH,
        )

    def taken(offset, part):
        origin = wrap(x - offset, SIDE)
        where = pl.ds(*parts[part])
        return pltpu.make_async_remote_copy(
            src_ref=made.at[origin, :, where],
            dst_ref=back.at[origin, :, where],
            send_sem=swap_send.at[offset, part],
            recv_sem=swap_recv.at[offset, part],
            device_id=(origin, strip),
            device_id_type=MESH,
        )

    def halo(offset, way):
        outgoing, incoming, to = ((top, below, up), (bottom, above, down))[way]
        return pltpu.make_async_remote_copy(
            src_ref=outgoing.at[offset],
            dst_ref=incoming.at[offset],
            send_sem=halo_send.at[offset, way],
            recv_sem=halo_recv.at[offset, way],
            device_id=(x, to),
            device_id_type=MESH,
        )

    def forward(offset):
        chan = wrap(x - offset, SIDE)
        if offset:
            taken(offset, 0).wait_recv()
            taken(offset, 1).wait_recv()
        for way, target in ((0, top), (1, bottom)):
            where = slice(parts[way][0], parts[way][0] + width)
            held = back if offset else made
            edge = frames[chan, :, where].astype(F32) - held[chan, :, where].astype(F32)
            ok = jnp.where(chan == side - 1, valid[:, where].astype(F32), 1.0)
            target[offset] = (edge * ok).astype(BF16)
        for way in range(2):
            halo(offset, way).start()

    multiply(0)
    multiply(1)
    for offset in (1, 3):
        for part in range(2):
            send(offset, part).start()
    forward(0)
    multiply(2)
    for offset in (1, 3):
        send(offset, 2).start()
    for part in (0, 1, 2):
        send(2, part).start()
    mine = pltpu.make_async_copy(made.at[x], back.at[x], local_sem)
    mine.start()
    mine.wait()

    def group(k, carry):
        offset = k + jnp.where(k == 2, 1, 0) - jnp.where(k == 3, 1, 0)

        @pl.when(k > 0)
        def _():
            taken(offset, 2).wait_recv()

        def edges_here():
            for way in range(2):
                halo(offset, way).wait_recv()

        def between(sweep):
            for turn, at, offsets in ((0, 3, (1, 3)), (2, 1, (2,))):
                if sweep == at:

                    @pl.when(k == turn)
                    def _():
                        for offset in offsets:
                            forward(offset)

        smooth_channel(
            strips, strip, wrap(x - offset, SIDE), offset, lam_ref,
            frames, back, valid, above, below, back_out, fore_out, lines_out,
            source, first, second, edges_here, between,
        )
        return carry

    lax.fori_loop(0, SIDE, group, 0)
    for offset in ORDER:
        for part in range(3):
            send(offset, part).wait_send()
    for offset in range(SIDE):
        for way in range(2):
            halo(offset, way).wait_send()


def whole_kernel(
    nval, lam_hbm, frames_hbm, prev_hbm, depth_hbm, sketch_hbm, back, fore, lam_ref, small_sem,
    *scratch
):
    swapped, flat_frames, flat_valid = scratch[:3]
    basis_sc = scratch[22]
    small = [
        pltpu.make_async_copy(lam_hbm, lam_ref, small_sem.at[0]),
        pltpu.make_async_copy(sketch_hbm, basis_sc, small_sem.at[1]),
    ]
    for copy in small:
        copy.start()
    gram = gram_stage(frames_hbm, prev_hbm, depth_hbm, *scratch[:21])
    for copy in small:
        copy.wait()
    mix = mixing_stage(gram * (1.0 / nval), *scratch[21:23])
    finish_stage(
        lam_ref, swapped, mix, flat_frames, flat_valid, back, fore, scratch[7], *scratch[23:]
    )


def low_rank_and_rest(frames, prev_fg, depth_valid, sketch, lam, nval):
    count, chans, rows, cols = frames.shape
    pixels = rows * cols
    every = count * SIDE
    piece = every // 8
    rank = sketch.shape[1]
    dma = pltpu.SemaphoreType.DMA
    flat = (chans, count, pixels)
    edge = (chans, count, NSWEEP * cols)
    field = (rows + 2 * NSWEEP, count, cols)
    gram_scratch = [
        VMEM(flat, BF16),
        VMEM(flat, BF16),
        VMEM((count, pixels), BF16),
        VMEM(frames.shape, BF16),
        VMEM(frames.shape, BF16),
        VMEM(depth_valid.shape, jnp.int32),
        VMEM(flat, BF16),
        VMEM((cols // 128, count * rows, 128), F32),
        VMEM((8, piece, every), F32),
        VMEM((8, piece, every), F32),
        VMEM((16, piece, every), F32),
        VMEM((8, piece, every), F32),
        dma((2 * chans + 1,)),
        dma((4, 2)), dma((4, 2)),
        dma((8,)), dma((8,)),
        dma((16,)), dma((16,)),
        dma((8,)), dma((8,)),
    ]
    mixing_scratch = [VMEM((every, every), F32), VMEM((rank, every), F32)]
    finish_scratch = [
        VMEM(flat, BF16),
        VMEM(flat, BF16),
        VMEM(edge, BF16),
        VMEM(edge, BF16),
        VMEM(edge, BF16),
        VMEM(edge, BF16),
        VMEM(field, F32),
        VMEM(field, F32),
        VMEM(field, F32),
        dma,
        dma((4, 3)), dma((4, 3)),
        dma((4, 2)), dma((4, 2)),
    ]
    return pl.pallas_call(
        functools.partial(whole_kernel, nval),
        out_shape=(jax.ShapeDtypeStruct(frames.shape, BF16),) * 2,
        in_specs=[pl.BlockSpec(memory_space=pltpu.HBM)] * 5,
        out_specs=tuple(in_vmem(2)),
        scratch_shapes=[pltpu.SMEM((chans,), F32), dma((2,))]
        + gram_scratch
        + mixing_scratch
        + finish_scratch,
        compiler_params=pltpu.CompilerParams(
            collective_id=0, has_side_effects=True, vmem_limit_bytes=48 << 20
        ),
        name="godec",
    )(*[pltpu.with_memory_space_constraint(v, pltpu.HBM) for v in (lam, frames, prev_fg, depth_valid, sketch.T)])


def local(frames, prev_fg, depth_valid, sketch, tv_weight):
    count, chans, rows, cols = frames.shape
    strips = lax.axis_size("pix")
    nval = chans * rows * strips * cols
    return low_rank_and_rest(frames, prev_fg, depth_valid, sketch, tv_weight, nval)


def solution(mesh):
    placed = (
        P("frame", None, "pix", None),
        P("frame", None, "pix", None),
        P("frame", "pix", None),
        P(),
        P(),
    )
    return jax.shard_map(
        local,
        mesh=mesh,
        in_specs=placed,
        out_specs=(P("frame", None, "pix", None), P("frame", None, "pix", None)),
        check_vma=False,
    )
```

```python
import functools

import jax
import jax.numpy as jnp
from jax import lax
from jax.experimental import pallas as pl
from jax.experimental.pallas import tpu as pltpu
from jax.sharding import PartitionSpec as P

POWER = 3
NSWEEP = 5
STEP_SIZE = 0.125
MESH = pl.DeviceIdType.MESH
VMEM = pltpu.VMEM
SIDE = 4
BF16 = jnp.bfloat16
F32 = jnp.float32


def in_vmem(count):
    return [pl.BlockSpec(memory_space=pltpu.VMEM)] * count


def wrap(value, size):
    return lax.rem(value + size, size)


def place():
    x = lax.axis_index("frame")
    strip = lax.axis_index("pix")
    return x, strip, lax.div(strip, 8), lax.rem(lax.div(strip, 2), 4), lax.rem(strip, 2)


def send_along_x(x, strip, src, dst, send_sem, recv_sem, offset, part, where):
    to = wrap(x + offset, SIDE)
    return pltpu.make_async_remote_copy(
        src_ref=src.at[to, :, where],
        dst_ref=dst.at[x, :, where],
        send_sem=send_sem.at[offset, part],
        recv_sem=recv_sem.at[offset, part],
        device_id=(to, strip),
        device_id_type=MESH,
    )


def taken_along_x(x, strip, src, dst, send_sem, recv_sem, offset, part, where):
    origin = wrap(x - offset, SIDE)
    return pltpu.make_async_remote_copy(
        src_ref=src.at[origin, :, where],
        dst_ref=dst.at[origin, :, where],
        send_sem=send_sem.at[offset, part],
        recv_sem=recv_sem.at[offset, part],
        device_id=(origin, strip),
        device_id_type=MESH,
    )


ORDER = (2, 1, 3)


def lay(lines, start, value):
    count, rows, cols = value.shape
    value = value.reshape(count * rows, cols)
    for j in range(lines.shape[0]):
        lines[j, start * rows : (start + count) * rows, :] = value[:, 128 * j : 128 * j + 128]


def turned(lines, write, rows):
    tiles, size, _ = lines.shape
    for r in range(rows):
        for j in range(tiles):
            start = (r * tiles + j) * 128
            value = lines.at[j][pl.ds(r, size // rows, stride=rows), :]
            write(slice(start, start + 128), value)


def gram_stage(
    frames_hbm, prev_hbm, depth_hbm, swapped, flat_frames, flat_valid, frames, prev, depth, flat, lines, part, pieces, in_plane, total,
    load_sem, swap_send, swap_recv, first_send, first_recv, plane_send, plane_recv,
    last_send, last_recv,
):
    x, strip, y, z, core = place()
    group = x * 2 + core
    count, chans, rows, cols = frames.shape
    channels = [wrap(x + offset, SIDE) for offset in ORDER + (0,)]
    loads = []
    first = pltpu.make_async_copy(depth_hbm, depth, load_sem.at[2 * chans])
    first.start()
    for k, chan in enumerate(channels):
        pair = [
            pltpu.make_async_copy(hbm.at[:, chan], vmem.at[:, chan], load_sem.at[2 * k + j])
            for j, (hbm, vmem) in enumerate(((frames_hbm, frames), (prev_hbm, prev)))
        ]
        for copy in pair:
            copy.start()
        loads.append(pair)

    def of_group(k):
        return (lax.div(k, 2), strip - core + lax.rem(k, 2))

    plane = y * 4 + z

    def of_plane(k):
        return (x, k * 2 + core)

    partners = [of_group(wrap(group + k, 8)) for k in range(1, 8)]
    partners += [of_plane(wrap(plane + k, 16)) for k in range(1, 16)]
    strips = lax.axis_size("pix")
    partners += [(x, wrap(strip + k, strips)) for k in (-1, 1)]
    barrier = pltpu.get_barrier_semaphore()
    for partner in partners:
        pl.semaphore_signal(barrier, inc=1, device_id=partner, device_id_type=MESH)

    def residual(chan, write):
        for f in range(0, count, 8):
            ok = jnp.where(chan == chans - 1, depth[f : f + 8].astype(F32), 1.0)
            value = (
                frames[f : f + 8, chan].astype(F32) - prev[f : f + 8, chan].astype(F32)
            ) * ok
            lay(lines, f, value)
        turned(lines, write, rows)

    args = (x, strip, flat, swapped, swap_send, swap_recv)
    pixels = rows * cols
    count_parts = 4
    span = pixels // count_parts
    halves = [pl.ds(k * span, span) for k in range(count_parts)]
    sends = []
    first.wait()
    for k, offset in enumerate(ORDER):
        for copy in loads[k]:
            copy.wait()

        def write(where, value, chan=channels[k]):
            flat[chan, :, where] = value.astype(BF16)

        residual(channels[k], write)
        if k == 0:
            pl.semaphore_wait(barrier, len(partners))
        sends.append(send_along_x(*args, offset, 0, halves[0]))
        sends[-1].start()
    for part_of in range(1, count_parts):
        for offset in ORDER:
            sends.append(send_along_x(*args, offset, part_of, halves[part_of]))
            sends[-1].start()
    for copy in loads[-1]:
        copy.wait()

    def write_own(where, value):
        swapped[x, :, where] = value.astype(BF16)

    residual(x, write_own)

    def write_valid(where, value):
        flat_valid[:, where] = value.astype(BF16)

    lay(lines, 0, depth[...].astype(F32))
    turned(lines, write_valid, rows)
    for chan in range(chans):

        def write_frames(where, value):
            flat_frames[chan, :, where] = value.astype(BF16)

        for f in range(0, count, 8):
            lay(lines, f, frames[f : f + 8, chan].astype(F32))
        turned(lines, write_frames, rows)
    every = count * SIDE
    chunk = 1024
    partial = jnp.zeros((every, every), F32)
    for half in range(count_parts):
        for offset in ORDER:
            taken_along_x(*args, offset, half, halves[half]).wait_recv()
        for start in range(half * span, (half + 1) * span, chunk):
            block = swapped[:, :, start : start + chunk].reshape(every, chunk)
            partial = partial + lax.dot_general(
                block, block, (((1,), (1,)), ((), ())), preferred_element_type=F32
            )
    for copy in sends:
        copy.wait_send()
    part[...] = partial.reshape(part.shape)

    def exchange(index, size, where, source_of, buffer, send_sem, recv_sem):
        copies = []
        for k in range(1, size):
            to = wrap(index + k, size)
            copies.append(
                pltpu.make_async_remote_copy(
                    src_ref=source_of(to),
                    dst_ref=buffer.at[index],
                    send_sem=send_sem.at[k],
                    recv_sem=recv_sem.at[k],
                    device_id=where(to),
                    device_id_type=MESH,
                )
            )
        for copy in copies:
            copy.start()
        return copies

    def arrive(index, size, where, source_of, buffer, send_sem, recv_sem, copies):
        for k in range(1, size):
            pltpu.make_async_remote_copy(
                src_ref=source_of(wrap(index + k, size)),
                dst_ref=buffer.at[wrap(index - k, size)],
                send_sem=send_sem.at[k],
                recv_sem=recv_sem.at[k],
                device_id=where(wrap(index + k, size)),
                device_id_type=MESH,
            ).wait_recv()
        for copy in copies:
            copy.wait_send()

    def added(buffer, size):
        out = buffer[0]
        for k in range(1, size):
            out = out + buffer[k]
        return out

    args = (group, 8, of_group, lambda k: part.at[k], pieces, first_send, first_recv)
    copies = exchange(*args)
    pieces[group] = part[group]
    arrive(*args, copies)
    in_plane[plane] = added(pieces, 8)

    args = (plane, 16, of_plane, lambda k: in_plane.at[plane], in_plane, plane_send, plane_recv)
    arrive(*args, exchange(*args))
    total[group] = added(in_plane, 16)

    args = (group, 8, of_group, lambda k: total.at[group], total, last_send, last_recv)
    arrive(*args, exchange(*args))
    return total[...].reshape(every, every)


def exact(left, right, dims):
    return lax.dot_general(
        left, right, (dims, ((), ())), precision=lax.Precision.HIGHEST, preferred_element_type=F32
    )


def lower_solve(square, sides):
    size = square.shape[0]
    blocks = size // 8
    sub = lax.broadcasted_iota(jnp.int32, (8, 128), 0)
    tiles = [square[8 * i : 8 * i + 8, :] for i in range(blocks)]
    hands = [[side[8 * i : 8 * i + 8, :] for i in range(blocks)] for side in sides]
    solved = [[] for _ in sides]
    for b in range(blocks):
        cols = [
            [
                jnp.broadcast_to(tiles[i][:, 8 * b + t : 8 * b + t + 1], (8, 128))
                if i >= b
                else None
                for i in range(blocks)
            ]
            for t in range(8)
        ]
        pivot = [
            [
                jnp.broadcast_to(cols[t][b][u : u + 1, :], (8, 128)) if u >= t else None
                for u in range(8)
            ]
            for t in range(8)
        ]
        rate = []
        low = [[None] * 8 for _ in range(8)]
        for t in range(8):
            rate.append(lax.rsqrt(pivot[t][t]))
            for u in range(t + 1, 8):
                low[u][t] = pivot[t][u] * rate[t]
            for u in range(t + 1, 8):
                for v in range(u, 8):
                    pivot[u][v] = pivot[u][v] - low[u][t] * low[v][t]

        def reduced(rows):
            done = []
            for t in range(8):
                value = rows[t]
                for s in range(t):
                    value = value - done[s] * low[t][s][:, : value.shape[1]]
                done.append(value * rate[t][:, : value.shape[1]])
            return done

        below = {i: reduced([cols[t][i] for t in range(8)]) for i in range(b + 1, blocks)}
        if b + 1 < blocks:
            across = reduced(
                [jnp.broadcast_to(tiles[b][t : t + 1, :], (8, size)) for t in range(8)]
            )
            for i in range(b + 1, blocks):
                for t in range(8):
                    tiles[i] = tiles[i] - below[i][t][:, :size] * across[t]
        for hand, out in zip(hands, solved):
            rows = reduced([jnp.broadcast_to(hand[b][t : t + 1, :], (8, 128)) for t in range(8)])
            tile = rows[0]
            for t in range(1, 8):
                tile = jnp.where(sub == t, rows[t], tile)
            out.append(tile)
            for i in range(b + 1, blocks):
                for t in range(8):
                    hand[i] = hand[i] - below[i][t] * rows[t]
    return [jnp.concatenate(out, axis=0) for out in solved]


def mixing_stage(gram, gram_sc, basis_sc):
    gram_sc[...] = gram

    def turn(step, carry):
        basis = basis_sc[...]
        image = exact(basis, gram_sc[...], ((1,), (1,)))
        square = exact(basis, image, ((1,), (1,)))
        basis_sc[...] = lower_solve(square, [image])[0]
        return carry

    lax.fori_loop(0, POWER, turn, 0)
    basis = basis_sc[...]
    image = exact(basis, gram_sc[...], ((1,), (0,)))
    square = exact(basis, image, ((1,), (1,)))
    left, right = lower_solve(square, [basis, image])
    return exact(right, left, ((0,), (0,))).astype(BF16)


def smooth_channel(
    strips, strip, chan, offset, lam_ref, frames, back, valid, above, below,
    back_out, fore_out, lines_out, source, first, second, edges_here, between,
):
    lam = lam_ref[chan]
    step = STEP_SIZE / lam
    last = frames.shape[0] - 1
    halo = NSWEEP
    span, lines, cols = source.shape
    rows = span - 2 * halo
    tiles = cols // 128
    lane = lax.broadcasted_iota(jnp.int32, (lines, 128), 1)
    open_above = jnp.where(strip > 0, F32(1.0), F32(0.0))
    open_below = jnp.where(strip < strips - 1, F32(1.0), F32(0.0))

    def tile(ref, r):
        return [ref[r, :, 128 * j : 128 * j + 128] for j in range(tiles)]

    def put(ref, r, values):
        for j in range(tiles):
            ref[r, :, 128 * j : 128 * j + 128] = values[j]

    def unturn(r, values):
        for j in range(tiles):
            lines_out.at[j][pl.ds(r, lines, stride=rows), :] = values[j]

    def unlay(target):
        for j in range(tiles):
            value = lines_out[j].reshape(lines, rows, 128).astype(BF16)
            target[:, chan, :, 128 * j : 128 * j + 128] = value

    for r in range(rows):
        where = slice(r * cols, (r + 1) * cols)
        ok = jnp.where(chan == last, valid[:, where].astype(F32), 1.0)
        held = back[chan, :, where].astype(F32)
        unturn(r, [held[:, 128 * j : 128 * j + 128] for j in range(tiles)])
        source[halo + r] = (frames[chan, :, where].astype(F32) - held) * (ok * step)
    unlay(back_out)
    edges_here()
    for r in range(halo):
        source[r] = above[offset, :, r * cols : (r + 1) * cols].astype(F32) * step
        source[halo + rows + r] = below[offset, :, r * cols : (r + 1) * cols].astype(F32) * step

    def before(values):
        turned = [pltpu.roll(v, 1, 1) for v in values]
        return [jnp.where(lane == 0, turned[j - 1] if j else 0.0, turned[j]) for j in range(tiles)]

    def after(values):
        turned = [pltpu.roll(v, 127, 1) for v in values]
        return [jnp.where(lane == 127, turned[j + 1] if j + 1 < tiles else values[j], turned[j]) for j in range(tiles)]

    def image(r, up, here, beside):
        left = before(beside)
        return [s - STEP_SIZE * ((h - u) + (b - l)) for s, u, h, b, l in zip(tile(source, r), up, here, beside, left)]

    def update(r, smooth, under, here, beside):
        right = after(smooth)
        news = []
        for j in range(tiles):
            down = under[j] - smooth[j]
            if r == halo - 1:
                down = down * open_above
            if r == halo + rows - 1:
                down = down * open_below
            across = right[j] - smooth[j]
            square = jnp.maximum(down * down + across * across, 1e-37)
            rate = 1.0 / (1.0 + square * lax.rsqrt(square))
            a = -down if here is None else here[j] - down
            b = -across if beside is None else beside[j] - across
            news.append((a * rate, b * rate))
        put(first, r, [n[0] for n in news])
        put(second, r, [n[1] for n in news])

    smooth = tile(source, 0)
    for r in range(span - 1):
        under = tile(source, r + 1)
        update(r, smooth, under, None, None)
        smooth = under
    for sweep in range(1, NSWEEP):
        between(sweep)
        here, beside = tile(first, sweep), tile(second, sweep)
        smooth = image(sweep, tile(first, sweep - 1), here, beside)
        for r in range(sweep, span - 1 - sweep):
            next_here, next_beside = tile(first, r + 1), tile(second, r + 1)
            under = image(r + 1, here, next_here, next_beside)
            update(r, smooth, under, here, beside)
            smooth, here, beside = under, next_here, next_beside
    for r in range(rows):
        i = halo + r
        values = image(i, tile(first, i - 1), tile(first, i), tile(second, i))
        unturn(r, [v * (lam * (1.0 / STEP_SIZE)) for v in values])
    unlay(fore_out)


def finish_stage(
    lam_ref, swapped, mix, frames, valid, back_out, fore_out, lines_out,
    back, made, top, bottom, above, below, source, first, second,
    local_sem, swap_send, swap_recv, halo_send, halo_recv,
):
    x, strip, _, _, _ = place()
    strips = lax.axis_size("pix")
    up, down = wrap(strip - 1, strips), wrap(strip + 1, strips)
    side, count, pixels = swapped.shape
    width = top.shape[-1]
    cols = source.shape[-1]
    parts = ((0, width), (pixels - width, width), (width, pixels - 2 * width))

    def multiply(part):
        start, size = parts[part]
        for at in range(start, start + size, 512):
            where = slice(at, at + 512)
            block = swapped[:, :, where].reshape(side * count, 512)
            out = jnp.dot(mix, block, preferred_element_type=F32)
            made[:, :, where] = out.astype(BF16).reshape(side, count, 512)

    def send(offset, part):
        to = wrap(x + offset, SIDE)
        where = pl.ds(*parts[part])
        return pltpu.make_async_remote_copy(
            src_ref=made.at[to, :, where],
            dst_ref=back.at[x, :, where],
            send_sem=swap_send.at[offset, part],
            recv_sem=swap_recv.at[offset, part],
            device_id=(to, strip),
            device_id_type=MESH,
        )

    def taken(offset, part):
        origin = wrap(x - offset, SIDE)
        where = pl.ds(*parts[part])
        return pltpu.make_async_remote_copy(
            src_ref=made.at[origin, :, where],
            dst_ref=back.at[origin, :, where],
            send_sem=swap_send.at[offset, part],
            recv_sem=swap_recv.at[offset, part],
            device_id=(origin, strip),
            device_id_type=MESH,
        )

    def halo(offset, way):
        outgoing, incoming, to = ((top, below, up), (bottom, above, down))[way]
        return pltpu.make_async_remote_copy(
            src_ref=outgoing.at[offset],
            dst_ref=incoming.at[offset],
            send_sem=halo_send.at[offset, way],
            recv_sem=halo_recv.at[offset, way],
            device_id=(x, to),
            device_id_type=MESH,
        )

    def forward(offset):
        chan = wrap(x - offset, SIDE)
        if offset:
            taken(offset, 0).wait_recv()
            taken(offset, 1).wait_recv()
        for way, target in ((0, top), (1, bottom)):
            where = slice(parts[way][0], parts[way][0] + width)
            held = back if offset else made
            edge = frames[chan, :, where].astype(F32) - held[chan, :, where].astype(F32)
            ok = jnp.where(chan == side - 1, valid[:, where].astype(F32), 1.0)
            target[offset] = (edge * ok).astype(BF16)
        for way in range(2):
            halo(offset, way).start()

    multiply(0)
    multiply(1)
    for offset in (1, 3):
        for part in range(2):
            send(offset, part).start()
    forward(0)
    multiply(2)
    for offset in (1, 3):
        send(offset, 2).start()
    for part in (0, 1, 2):
        send(2, part).start()
    mine = pltpu.make_async_copy(made.at[x], back.at[x], local_sem)
    mine.start()
    mine.wait()

    def group(k, carry):
        offset = k + jnp.where(k == 2, 1, 0) - jnp.where(k == 3, 1, 0)

        @pl.when(k > 0)
        def _():
            taken(offset, 2).wait_recv()

        def edges_here():
            for way in range(2):
                halo(offset, way).wait_recv()

        def between(sweep):
            for turn, at, offsets in ((0, 3, (1, 3)), (2, 1, (2,))):
                if sweep == at:

                    @pl.when(k == turn)
                    def _():
                        for offset in offsets:
                            forward(offset)

        smooth_channel(
            strips, strip, wrap(x - offset, SIDE), offset, lam_ref,
            frames, back, valid, above, below, back_out, fore_out, lines_out,
            source, first, second, edges_here, between,
        )
        return carry

    lax.fori_loop(0, SIDE, group, 0)
    for offset in ORDER:
        for part in range(3):
            send(offset, part).wait_send()
    for offset in range(SIDE):
        for way in range(2):
            halo(offset, way).wait_send()


def whole_kernel(
    nval, lam_hbm, frames_hbm, prev_hbm, depth_hbm, sketch_hbm, back, fore, lam_ref, small_sem,
    *scratch
):
    swapped, flat_frames, flat_valid = scratch[:3]
    basis_sc = scratch[22]
    small = [
        pltpu.make_async_copy(lam_hbm, lam_ref, small_sem.at[0]),
        pltpu.make_async_copy(sketch_hbm, basis_sc, small_sem.at[1]),
    ]
    for copy in small:
        copy.start()
    gram = gram_stage(frames_hbm, prev_hbm, depth_hbm, *scratch[:21])
    for copy in small:
        copy.wait()
    mix = mixing_stage(gram * (1.0 / nval), *scratch[21:23])
    finish_stage(
        lam_ref, swapped, mix, flat_frames, flat_valid, back, fore, scratch[7], *scratch[23:]
    )


def low_rank_and_rest(frames, prev_fg, depth_valid, sketch, lam, nval):
    count, chans, rows, cols = frames.shape
    pixels = rows * cols
    every = count * SIDE
    piece = every // 8
    rank = sketch.shape[1]
    dma = pltpu.SemaphoreType.DMA
    flat = (chans, count, pixels)
    edge = (chans, count, NSWEEP * cols)
    field = (rows + 2 * NSWEEP, count, cols)
    gram_scratch = [
        VMEM(flat, BF16),
        VMEM(flat, BF16),
        VMEM((count, pixels), BF16),
        VMEM(frames.shape, BF16),
        VMEM(frames.shape, BF16),
        VMEM(depth_valid.shape, jnp.int32),
        VMEM(flat, BF16),
        VMEM((cols // 128, count * rows, 128), F32),
        VMEM((8, piece, every), F32),
        VMEM((8, piece, every), F32),
        VMEM((16, piece, every), F32),
        VMEM((8, piece, every), F32),
        dma((2 * chans + 1,)),
        dma((4, 4)), dma((4, 4)),
        dma((8,)), dma((8,)),
        dma((16,)), dma((16,)),
        dma((8,)), dma((8,)),
    ]
    mixing_scratch = [VMEM((every, every), F32), VMEM((rank, every), F32)]
    finish_scratch = [
        VMEM(flat, BF16),
        VMEM(flat, BF16),
        VMEM(edge, BF16),
        VMEM(edge, BF16),
        VMEM(edge, BF16),
        VMEM(edge, BF16),
        VMEM(field, F32),
        VMEM(field, F32),
        VMEM(field, F32),
        dma,
        dma((4, 3)), dma((4, 3)),
        dma((4, 2)), dma((4, 2)),
    ]
    return pl.pallas_call(
        functools.partial(whole_kernel, nval),
        out_shape=(jax.ShapeDtypeStruct(frames.shape, BF16),) * 2,
        in_specs=[pl.BlockSpec(memory_space=pltpu.HBM)] * 5,
        out_specs=tuple(in_vmem(2)),
        scratch_shapes=[pltpu.SMEM((chans,), F32), dma((2,))]
        + gram_scratch
        + mixing_scratch
        + finish_scratch,
        compiler_params=pltpu.CompilerParams(
            collective_id=0, has_side_effects=True, vmem_limit_bytes=48 << 20
        ),
        name="godec",
    )(*[pltpu.with_memory_space_constraint(v, pltpu.HBM) for v in (lam, frames, prev_fg, depth_valid, sketch.T)])


def local(frames, prev_fg, depth_valid, sketch, tv_weight):
    count, chans, rows, cols = frames.shape
    strips = lax.axis_size("pix")
    nval = chans * rows * strips * cols
    return low_rank_and_rest(frames, prev_fg, depth_valid, sketch, tv_weight, nval)


def solution(mesh):
    placed = (
        P("frame", None, "pix", None),
        P("frame", None, "pix", None),
        P("frame", "pix", None),
        P(),
        P(),
    )
    return jax.shard_map(
        local,
        mesh=mesh,
        in_specs=placed,
        out_specs=(P("frame", None, "pix", None), P("frame", None, "pix", None)),
        check_vma=False,
    )
```
